128 devices in a mesh: gx: 32 (over y, z_lo, x), gy: 4 (over z_hi, core).
Axes of the slice: x: 4, y: 4, z: 4 (z_hi: 2, z_lo: 2; z = z_hi * 2 + z_lo), core: 2. Of those that a mesh axis runs over, the one named last changes fastest.
Arguments:
- control: float32 [4, 4096, 1024], P(None, 'gx', 'gy'), may hold values from -6 to 6
- background_std: float32 [4, 4096, 1024], P(None, 'gx', 'gy'), may hold values from 0.5 to 2
- kappa_x: float32 [2, 4096, 1024], P(None, 'gx', 'gy'), may hold values from 0.02 to 0.24
- kappa_y: float32 [2, 4096, 1024], P(None, 'gx', 'gy'), may hold values from 0.02 to 0.24
- sea_mask: int32 [2, 4096, 1024], P(None, 'gx', 'gy'), may hold values 0 or 1
- obs_weights: bfloat16 [4096, 128, 256], P(('gx', 'gy')), may hold values from -0.375 to 0.375
- obs_values: float32 [4096, 128], P(('gx', 'gy')), may hold values from -6 to 6
- obs_rinv: float32 [4096, 128], P(('gx', 'gy')), may hold values from 0.5 to 2
- obs_tile: int32 [4096, 1], P(('gx', 'gy')), may hold values from 0 to 31; in each aligned block of 32 rows (0 to 31, 32 to 63, ...) at most 2 rows name the same one
- obs_offset: int32 [4096], P(('gx', 'gy')), may hold values from 0 to 511
Outputs:
- gradient: float32 [4, 4096, 1024], P(None, 'gx', 'gy')
- departures: float32 [4096, 128], P(('gx', 'gy'))
The draws below stay inside these ranges and needn't reach their ends.
Inputs may be any that keep to these rules, and one draw needn't show every extreme that they name: `obs_tile`: among the blocks of one device at most 2 name the same tile column, and on at least one device exactly 2 blocks name the same tile column.
All inputs are finite; a program needn't handle non-finite values. No bound on the sum of `sea_mask` on one device may be relied on, other than what follows from the above.
Results may differ from the reference program's by a relative error of at most 0.00086.
Values may be sent and summed in bfloat16 or wider, within the bound.
A program may use at most 128 MiB of HBM per device.

```python
import math
import jax
import jax.numpy as jnp
import numpy as np
from jax import lax

VARS = 2
LEV = 2
CX = 128
NSTEP = 8
SEG = 128
NOBS = 128
NBD = 32
NX = 4096
NY = 1024
PLANES = 4
NSEG = 2
NPATCH = 512
PW = 256
CAP = 2
NB = 4096
N_GX = 32
N_GY = 4


def touch_ends(result, own_key, low, top_value):
    place = [jax.random.randint(jax.random.fold_in(own_key, axis), (), 0, length) for axis, length in enumerate(result.shape)]
    widest = result.shape.index(max(result.shape))
    next_to = place[:widest] + [(place[widest] + 1) % result.shape[widest]] + place[widest + 1:]
    return result.at[tuple(place)].set(low).at[tuple(next_to)].set(top_value)


def level_of(stream_key, shape, cuts, low, top_value):
    def one(axis_at, blocks):
        steps = jax.random.uniform(jax.random.fold_in(jax.random.fold_in(stream_key, 6), axis_at), (blocks,), jnp.float32, low / len(cuts), top_value / len(cuts))
        return jnp.repeat(jnp.exp(steps), shape[axis_at] // blocks).reshape((-1,) + (1,) * (len(shape) - axis_at - 1))

    gain = one(*cuts[0])
    for cut in cuts[1:]:
        gain = gain * one(*cut)
    return gain


def assign_block(stream_key, own, number, rows, count, top, most, skew):
    order = jax.random.permutation(stream_key, count)
    packed, usual = shares(count, rows * top, most, skew, True), shares(count, rows * top, most, skew, False)
    places = jnp.arange(count)

    def named(tallies, turn):
        used = int((tallies > 0).sum())
        fixed = max(1, used // 4)
        shifted = fixed + (places - fixed + turn * (used - fixed)) % max(1, count - fixed)
        return jnp.zeros((count,), jnp.int32).at[order[jnp.where(places < fixed, places, shifted)]].set(jnp.asarray(tallies, jnp.int32))

    tallies = jnp.where(number % 4 == 0, named(packed, number // 4), named(usual, number - number // 4 - 1))
    mixed = jax.random.permutation(jax.random.fold_in(own, 3), count)
    donor, sink = mixed[0:count // 2 * 2:2], mixed[1:count // 2 * 2:2]
    margin = jnp.minimum(tallies[donor] - 1, most - tallies[sink]) // 2
    margin = jnp.where((donor == order[0]) | (sink == order[0]) | (tallies[sink] == 0), 0, jnp.maximum(margin, 0))
    shifted = jax.random.randint(jax.random.fold_in(own, 4), (count // 2,), 0, 1 << 20) % (margin + 1)
    tallies = tallies.at[donor].add(-shifted).at[sink].add(shifted)
    labels = jnp.searchsorted(jnp.cumsum(tallies), jnp.arange(rows * top), side="right").astype(jnp.int32)
    table = labels.reshape(top, rows).T
    table = table[jax.random.permutation(jax.random.fold_in(own, 1), rows)]
    turn = jax.random.randint(jax.random.fold_in(own, 2), (rows, 1), 0, top)
    return jnp.take_along_axis(table, (jnp.arange(top)[None, :] + turn) % top, axis=1)


def shares(number_of, total, reach, skew, full):
    weights = [(1 << 20) // math.isqrt(standing ** skew) + 1 for standing in range(1, number_of + 1)]
    largest = reach if full else min(reach, max(-(-total // number_of), total * weights[0] // sum(weights)))
    least = 1 if total - largest >= number_of - 1 else 0
    counts, rest = [largest] + [least] * (number_of - 1), total - largest - least * (number_of - 1)
    while rest > 0:
        candidates = [i for i in range(1, number_of) if counts[i] < largest] or [i for i in range(1, number_of) if counts[i] < reach]
        mass, remaining = sum([weights[i] for i in candidates]), rest
        for i in candidates:
            extra = min(reach - counts[i], max(1, remaining * weights[i] // mass), rest)
            counts[i] = counts[i] + extra
            rest = rest - extra
    return np.array(counts)


def centred(stream_key, dims, deviation, limit, split=(), held_as=jnp.bfloat16):
    level = level_of(stream_key, dims, split, -0.22, 0.18) if split else 1.0
    result = jax.random.normal(stream_key, dims, jnp.float32) * deviation * level
    return jnp.minimum(jnp.maximum(result, -limit), limit).astype(held_as)


def setup_inputs(seed: int = 0) -> dict:
    key_of = jax.random.split(jax.random.key(seed), 11)
    control = centred(key_of[0], (PLANES, NX, NY), 1.0, 6.0, ((1, 32), (2, 4)), jnp.float32)
    background_std = jnp.clip(jnp.exp(math.log(2.0) - 1.3862944 * jax.random.uniform(key_of[1], (PLANES, NX, NY), jnp.float32) ** level_of(key_of[1], (PLANES, NX, NY), ((1, 32), (2, 4)), -0.2, 0.2)), 0.5, 2.0)
    kappa_x = jnp.clip(0.02 + 0.22 * jax.random.uniform(key_of[2], (LEV, NX, NY), jnp.float32) ** level_of(key_of[2], (LEV, NX, NY), ((1, 32), (2, 4)), -0.2, 0.2), 0.02, 0.24)
    kappa_y = jnp.clip(0.02 + 0.22 * jax.random.uniform(key_of[3], (LEV, NX, NY), jnp.float32) ** level_of(key_of[3], (LEV, NX, NY), ((1, 32), (2, 4)), -0.2, 0.2), 0.02, 0.24)
    sea_mask = touch_ends((jax.random.randint(key_of[4], (LEV, NX, NY), 0, 10) < 9).astype(jnp.int32), jax.random.fold_in(key_of[4], 1), 0, 1)
    obs_weights = centred(key_of[5], (NB, NOBS, PW), PW ** -0.5, 0.375, ((0, 128),))
    obs_values = centred(key_of[6], (NB, NOBS), 1.0, 6.0, ((0, 128),), jnp.float32)
    obs_rinv = jnp.clip(jnp.exp(math.log(2.0) - 1.3862944 * jax.random.uniform(key_of[7], (NB, NOBS), jnp.float32) ** level_of(key_of[7], (NB, NOBS), ((0, 128),), -0.2, 0.2)), 0.5, 2.0)
    obs_tile_keys = jax.random.split(jax.random.fold_in(key_of[8], 1), NB // NBD)
    obs_tile_turns = jax.random.permutation(jax.random.fold_in(key_of[8], 3), NB // NBD)
    obs_tile = jax.vmap(lambda own, number: assign_block(jax.random.fold_in(key_of[8], 2), own, number, NBD, N_GX, 1, CAP, 2))(obs_tile_keys, obs_tile_turns).reshape((NB, 1))
    obs_offset = touch_ends(jax.random.randint(key_of[9], (NB,), 0, NPATCH), jax.random.fold_in(key_of[9], 1), 0, NPATCH - 1).astype(jnp.int32)
    return {"control": control, "background_std": background_std, "kappa_x": kappa_x, "kappa_y": kappa_y, "sea_mask": sea_mask, "obs_weights": obs_weights, "obs_values": obs_values, "obs_rinv": obs_rinv, "obs_tile": obs_tile, "obs_offset": obs_offset}


def diffuse_global(planes_in, face_x, face_y):
    west_face = jnp.roll(face_x, 1, axis=1)
    south_face = jnp.concatenate([jnp.zeros_like(face_y[:, :, :1]), face_y[:, :, :-1]], axis=2)
    cell_grid = planes_in.reshape(VARS, LEV, NX, NY)
    for step_index in range(NSTEP):
        zero_row = jnp.zeros_like(cell_grid[:, :, :, :1])
        north_cell = jnp.concatenate([cell_grid[:, :, :, 1:], zero_row], axis=3)
        south_cell = jnp.concatenate([zero_row, cell_grid[:, :, :, :-1]], axis=3)
        east_flux = face_x * (jnp.roll(cell_grid, -1, axis=2) - cell_grid)
        west_flux = west_face * (jnp.roll(cell_grid, 1, axis=2) - cell_grid)
        north_flux = face_y * (north_cell - cell_grid)
        south_flux = south_face * (south_cell - cell_grid)
        cell_grid = cell_grid + east_flux + west_flux + north_flux + south_flux
    return cell_grid.reshape(VARS * LEV, NX, NY)


def reference(control, background_std, kappa_x, kappa_y, sea_mask, obs_weights, obs_values, obs_rinv, obs_tile, obs_offset):
    sea_float = sea_mask.astype(jnp.float32)
    face_x = kappa_x * sea_float * jnp.roll(sea_float, -1, axis=1)
    above = jnp.concatenate([sea_float[:, :, 1:], jnp.zeros_like(sea_float[:, :, :1])], axis=2)
    face_y = kappa_y * sea_float * above
    sea_planes = jnp.concatenate([sea_float] * VARS, axis=0)
    state_field = background_std * diffuse_global(sea_planes * control, face_x, face_y)
    patch_rows = state_field.astype(jnp.bfloat16).reshape(VARS, LEV, N_GX, CX, N_GY, NSEG, SEG)
    patch_rows = patch_rows.transpose(2, 4, 1, 3, 5, 0, 6).reshape(N_GX * N_GY * NPATCH, PW)
    holder_row = ((jnp.arange(NB, dtype=jnp.int32) // NBD) % N_GY).astype(jnp.int32)
    patch_index = ((obs_tile[:, 0] * N_GY + holder_row) * NPATCH + obs_offset).astype(jnp.int32)
    patches = jnp.take(patch_rows, patch_index, axis=0)
    groups = N_GX * N_GY

    def per_group(items):
        weights_here, patch_here, values_here, rinv_here = items
        weights_wide = weights_here.astype(jnp.float32)
        equivalents = jnp.einsum("bop,bp->bo", weights_wide, patch_here.astype(jnp.float32))
        departed = rinv_here * (equivalents - values_here)
        low_dep = departed.astype(jnp.bfloat16).astype(jnp.float32)
        obs_terms = jnp.einsum("bop,bo->bp", weights_wide, low_dep)
        return departed, obs_terms

    departures, obs_terms = lax.map(per_group, (obs_weights.reshape(groups, NBD, NOBS, PW), patches.reshape(groups, NBD, PW), obs_values.reshape(groups, NBD, NOBS), obs_rinv.reshape(groups, NBD, NOBS)))
    departures = departures.reshape(NB, NOBS)
    obs_terms = obs_terms.reshape(NB, PW)
    forcing_rows = jax.ops.segment_sum(obs_terms, patch_index, num_segments=N_GX * N_GY * NPATCH)
    forcing = forcing_rows.reshape(N_GX, N_GY, LEV, CX, NSEG, VARS, SEG).transpose(5, 2, 0, 3, 1, 4, 6).reshape(VARS * LEV, NX, NY)
    gradient = control + sea_planes * diffuse_global(background_std * forcing, face_x, face_y)
    return gradient, departures
```

```python
import functools

import jax
import jax.numpy as jnp
from jax import lax
from jax.experimental import pallas as pl
from jax.experimental.pallas import tpu as pltpu
from jax.sharding import PartitionSpec as P

VARS = 2
NSTEP = 8
LANES = 128
RIM = 8
CAP = 2
TOP = 2 * RIM
CHUNK = 16
MESH = pl.DeviceIdType.MESH
F32 = jnp.float32
BF16 = jnp.bfloat16


def lane_iota(shape):
    return lax.broadcasted_iota(jnp.int32, shape, len(shape) - 1)


def row_iota(shape):
    return lax.broadcasted_iota(jnp.int32, shape, len(shape) - 2)


def north_of(tiles, last_lane):
    rolled = [pltpu.roll(tile, LANES - 1, 1) for tile in tiles]
    count = len(tiles)
    return [jnp.where(last_lane, rolled[(t + 1) % count], rolled[t]) for t in range(count)]


def south_of(tiles, first_lane):
    rolled = [pltpu.roll(tile, 1, 1) for tile in tiles]
    count = len(tiles)
    return [jnp.where(first_lane, rolled[(t - 1) % count], rolled[t]) for t in range(count)]


def diffuse_step(src, dst, fx, fy, levels, rows):
    ntile = src.shape[1]
    first_lane = lane_iota((CHUNK, LANES)) == 0
    last_lane = lane_iota((CHUNK, LANES)) == LANES - 1
    for level in range(levels):
        for base in range(RIM, RIM + rows + 2 * RIM, CHUNK):
            here, above, below = (
                pl.ds(base, CHUNK),
                pl.ds(base + 1, CHUNK),
                pl.ds(base - 1, CHUNK),
            )
            east = [fx[level, t, here, :] for t in range(ntile)]
            west = [fx[level, t, below, :] for t in range(ntile)]
            north = [fy[level, t, here, :] for t in range(ntile)]
            for var in range(VARS):
                plane = var * levels + level
                center = [src[plane, t, here, :] for t in range(ntile)]
                up = north_of(center, last_lane)
                flux = [north[t] * (up[t] - center[t]) for t in range(ntile)]
                back = south_of(flux, first_lane)
                for t in range(ntile):
                    cell = center[t]
                    dst[plane, t, here, :] = (
                        cell
                        + east[t] * (src[plane, t, above, :] - cell)
                        + west[t] * (src[plane, t, below, :] - cell)
                        + flux[t]
                        - back[t]
                    )


def diffuse(first, second, fx, fy, levels, rows):
    def twice(_, carry):
        diffuse_step(first, second, fx, fy, levels, rows)
        diffuse_step(second, first, fx, fy, levels, rows)
        return carry

    lax.fori_loop(0, NSTEP // 2, twice, 0)


def split_three(value):
    high = value.astype(BF16)
    rest = value - high.astype(F32)
    middle = rest.astype(BF16)
    low = (rest - middle.astype(F32)).astype(BF16)
    return high, middle, low


def exact_dot(ones, value):
    width = value.shape[1]
    parts = jnp.concatenate(split_three(value), axis=1)
    sums = jnp.dot(ones, parts, preferred_element_type=F32)
    return sums[:, :width] + sums[:, width : 2 * width] + sums[:, 2 * width :]


def kernel(
    n_x,
    n_y,
    control,
    background_std,
    kappa_x,
    kappa_y,
    sea_mask,
    obs_weights,
    obs_values,
    obs_rinv,
    tile_row,
    offset_row,
    gradient,
    departures,
    xin,
    sea_in,
    std,
    weights,
    sea,
    fx,
    fy,
    field_a,
    field_b,
    field_c,
    strip_out,
    strip_in,
    strip_out2,
    strip_in2,
    index_out,
    index_in,
    patch_out,
    patch_in,
    term_out,
    term_in,
    terms,
    out_tile,
    load_sem,
    x_send,
    x_recv,
    y_send,
    y_recv,
    x2_send,
    x2_recv,
    y2_send,
    y2_recv,
    all_send,
    all_recv,
):
    planes, rows, cols = control.shape
    levels = planes // VARS
    blocks = obs_values.shape[0]
    segs = cols // LANES
    ix, jy = lax.axis_index("gx"), lax.axis_index("gy")
    east, west = lax.rem(ix + 1, n_x), lax.rem(ix + n_x - 1, n_x)
    north, south = lax.rem(jy + 1, n_y), lax.rem(jy + n_y - 1, n_y)
    own = pl.ds(TOP, rows)
    low_rim, high_rim = pl.ds(RIM, RIM), pl.ds(TOP + rows, RIM)
    low_edge, high_edge = pl.ds(TOP, RIM), pl.ds(TOP + rows - RIM, RIM)
    ext = pl.ds(RIM, rows + 2 * RIM)
    ext_rows = rows + 2 * RIM
    height = rows + 4 * RIM

    barrier = pltpu.get_barrier_semaphore()

    def greet(step, carry):
        pl.semaphore_signal(
            barrier, inc=1, device_id=(lax.rem(ix + step, n_x), jy), device_id_type=MESH
        )
        return carry

    lax.fori_loop(1, n_x, greet, 0)
    for other_y in (north, south):
        for other_x in (west, ix, east):
            pl.semaphore_signal(
                barrier, inc=1, device_id=(other_x, other_y), device_id_type=MESH
            )

    loads = []

    def load(source, target):
        copy = pltpu.make_async_copy(source, target, load_sem.at[len(loads)])
        copy.start()
        loads.append(copy)

    for t in range(segs):
        span = pl.ds(t * LANES, LANES)
        load(sea_mask.at[:, :, span], sea_in.at[:, t, own, :])
        load(kappa_x.at[:, :, span], xin.at[pl.ds(planes, levels), t, own, :])
        load(kappa_y.at[:, :, span], xin.at[pl.ds(planes + levels, levels), t, own, :])
        load(control.at[:, :, span], xin.at[pl.ds(0, planes), t, own, :])
    late = len(loads)
    for t in range(segs):
        load(background_std.at[:, :, pl.ds(t * LANES, LANES)], std.at[:, t, :, :])
    load(obs_weights, weights)

    edge = jnp.zeros((RIM, LANES), F32)
    for ref in (field_a, field_b, field_c):
        for plane in range(planes):
            for t in range(segs + 1):
                ref[plane, t, pl.ds(0, RIM), :] = edge
                ref[plane, t, pl.ds(height - RIM, RIM), :] = edge
    for level in range(levels):
        for t in range(segs + 1):
            fx[level, t, pl.ds(0, RIM), :] = edge
            sea[level, t, pl.ds(height - RIM, RIM), :] = edge

    row = tile_row[...].astype(F32)
    pair = (blocks, blocks)
    diagonal = lane_iota(pair) == row_iota(pair)
    col = jnp.sum(jnp.where(diagonal, row, 0.0), axis=1, keepdims=True)
    same = col == row
    rank_col = jnp.max(
        jnp.where(same & (lane_iota(pair) < row_iota(pair)), 1.0, 0.0), axis=1, keepdims=True
    )
    rank_row = jnp.max(
        jnp.where(same & (row_iota(pair) < lane_iota(pair)), 1.0, 0.0), axis=0, keepdims=True
    )
    slots = CAP * n_x
    slot_lane = lane_iota((blocks, slots))
    late_lane = slot_lane >= n_x
    block_slot = jnp.where(
        (jnp.where(late_lane, slot_lane - n_x, slot_lane).astype(F32) == col)
        & (jnp.where(late_lane, 1.0, 0.0) == rank_col),
        1.0,
        0.0,
    ).astype(BF16)
    slot_row = row_iota((slots, blocks))
    late_row = slot_row >= n_x
    slot_block = jnp.where(
        (jnp.where(late_row, slot_row - n_x, slot_row).astype(F32) == row)
        & (jnp.where(late_row, 1.0, 0.0) == rank_row),
        1.0,
        0.0,
    )
    wanted = (
        jnp.sum(slot_block * (offset_row[...].astype(F32) + 1.0), axis=1, keepdims=True) - 1.0
    )
    wanted = jnp.broadcast_to(wanted, (slots, LANES))
    for c in range(CAP):
        index_out[:, 0, pl.ds(c * LANES, LANES)] = wanted[c * n_x : (c + 1) * n_x]

    for copy in loads[:late]:
        copy.wait()
    strip_lane = lane_iota((rows, LANES))
    for side, t in ((0, 0), (1, segs - 1)):
        strip = jnp.zeros((rows, LANES), F32)
        for index in range(planes + 2 * levels):
            level = index % levels
            value = jnp.where(sea_in[level, t, own, :] > 0, xin[index, t, own, :], 0.0)
            shift = (index * RIM + side * RIM) % LANES
            if shift:
                value = pltpu.roll(value, shift, 1)
            here = (strip_lane >= index * RIM) & (strip_lane < (index + 1) * RIM)
            strip = jnp.where(here, value, strip)
        strip_out[side] = strip

    pl.semaphore_wait(barrier, n_x - 1 + 6)

    def send(source, target, sems, number, device):
        copy = pltpu.make_async_remote_copy(
            source,
            target,
            sems[0].at[number],
            sems[1].at[number],
            device_id=device,
            device_id_type=MESH,
        )
        copy.start()
        return copy

    def send_x(refs, sems):
        return [
            send(
                ref.at[:, pl.ds(0, segs), edge_rows, :],
                ref.at[:, pl.ds(0, segs), rim_rows, :],
                sems,
                2 * number + side,
                (other, jy),
            )
            for number, ref in enumerate(refs)
            for side, edge_rows, rim_rows, other in (
                (0, low_edge, high_rim, west),
                (1, high_edge, low_rim, east),
            )
        ]

    def send_y(source, target, sems):
        copies = []
        for side, other_y in ((0, south), (1, north)):
            for number, from_rows, to_rows, other_x in (
                (0, pl.ds(0, rows), own, ix),
                (1, pl.ds(0, RIM), high_rim, west),
                (2, pl.ds(rows - RIM, RIM), low_rim, east),
            ):
                copies.append(
                    send(
                        source.at[side, from_rows, :],
                        target.at[1 - side, to_rows, :],
                        sems,
                        3 * side + number,
                        (other_x, other_y),
                    )
                )
        return copies

    def send_all(source, target, number):
        def one(step, carry):
            other = lax.rem(ix + step, n_x)
            pltpu.make_async_remote_copy(
                source.at[other],
                target.at[ix],
                all_send.at[number],
                all_recv.at[number],
                device_id=(other, jy),
                device_id_type=MESH,
            ).start()
            return carry

        lax.fori_loop(1, n_x, one, 0)
        target[pl.ds(ix, 1)] = source[pl.ds(ix, 1)]
        return pltpu.make_async_remote_copy(
            source.at[pl.ds(0, n_x - 1)],
            target.at[pl.ds(0, n_x - 1)],
            all_send.at[number],
            all_recv.at[number],
            device_id=(east, jy),
            device_id_type=MESH,
        )

    sent_y = send_y(strip_out, strip_in, (y_send, y_recv))
    sent_x = send_x((xin, sea_in), (x_send, x_recv))
    sent_index = send_all(index_out, index_in, 0)

    for copy in sent_x:
        copy.wait()
    for level in range(levels):
        for t in range(segs):
            wet = sea_in[level, t, ext, :] > 0
            sea[level, t, ext, :] = jnp.where(wet, 1.0, 0.0)
            fx[level, t, ext, :] = jnp.where(wet, xin[planes + level, t, ext, :], 0.0)
            fy[level, t, ext, :] = jnp.where(wet, xin[planes + levels + level, t, ext, :], 0.0)
            for var in range(VARS):
                plane = var * levels + level
                field_a[plane, t, ext, :] = jnp.where(wet, xin[plane, t, ext, :], 0.0)
    for copy in sent_y:
        copy.wait()
    ext_lane = lane_iota((ext_rows, LANES))
    from_low = (ext_lane >= LANES - RIM) & (jy > 0)
    from_high = (ext_lane < RIM) & (jy < n_y - 1)

    def unpack(strips, index):
        low = pltpu.roll(strips[0, ext, :], (LANES - RIM - index * RIM) % LANES, 1)
        high = strips[1, ext, :]
        if index:
            high = pltpu.roll(high, LANES - index * RIM, 1)
        return jnp.where(from_high, high, jnp.where(from_low, low, 0.0))

    for plane in range(planes):
        field_a[plane, segs, ext, :] = unpack(strip_in, plane)
    for level in range(levels):
        face = unpack(strip_in, planes + level)
        fx[level, segs, ext, :] = face
        sea[level, segs, ext, :] = jnp.where(face > 0.0, 1.0, 0.0)
        fy[level, segs, ext, :] = unpack(strip_in, planes + levels + level)
    last_lane = ext_lane == LANES - 1
    for level in range(levels):
        wet_north = north_of([sea[level, t, ext, :] for t in range(segs + 1)], last_lane)
        for t in range(segs + 1):
            fx[level, t, ext, :] = (
                fx[level, t, ext, :] * sea[level, t, pl.ds(RIM + 1, ext_rows), :]
            )
            fy[level, t, ext, :] = fy[level, t, ext, :] * wet_north[t]

    diffuse(field_a, field_b, fx, fy, levels, rows)

    for copy in loads[late:]:
        copy.wait()
    sent_index.wait()
    asked = jnp.concatenate(
        [index_in[:, 0, pl.ds(c * LANES, LANES)] for c in range(CAP)], axis=0
    )
    number = lane_iota((slots, LANES)) * segs
    if rows < LANES:
        number = jnp.where(number < rows * segs, number, -2)
    hits = jnp.concatenate(
        [
            jnp.where(asked == (number + (level * rows * segs + s)).astype(F32), 1.0, 0.0)
            for level in range(levels)
            for s in range(segs)
        ],
        axis=1,
    ).astype(BF16)
    table = jnp.concatenate(
        [
            jnp.concatenate(
                [
                    (std[v * levels + level, s] * field_a[v * levels + level, s, own, :]).astype(
                        BF16
                    )
                    for v in range(VARS)
                ],
                axis=1,
            )
            for level in range(levels)
            for s in range(segs)
        ],
        axis=0,
    )
    patch_width = VARS * LANES
    picked = jnp.dot(hits, table, preferred_element_type=F32)
    for c in range(CAP):
        patch_out[:, 0, pl.ds(c * patch_width, patch_width)] = picked[c * n_x : (c + 1) * n_x]
    sent_patch = send_all(patch_out, patch_in, 1)
    sent_patch.wait()
    arrived = jnp.concatenate(
        [patch_in[:, 0, pl.ds(c * patch_width, patch_width)] for c in range(CAP)], axis=0
    ).astype(BF16)
    patches = jnp.dot(block_slot, arrived, preferred_element_type=F32).astype(BF16)

    nobs = obs_values.shape[1]
    obs_lane = lane_iota((nobs, LANES))
    padded = jnp.concatenate(
        [patches, jnp.zeros((LANES - blocks, patch_width), BF16)], axis=0
    )

    def one_equivalent(b, total):
        product = lax.dot_general(
            weights[b], padded, (((1,), (1,)), ((), ())), preferred_element_type=F32
        )
        return jnp.where(obs_lane == b, product, total)

    equivalents = lax.fori_loop(0, blocks, one_equivalent, jnp.zeros((nobs, LANES), F32))
    departed = obs_rinv[...] * (equivalents.T[:blocks] - obs_values[...])
    departures[...] = departed
    low = departed.astype(BF16).astype(F32)
    low_cols = jnp.concatenate([low, jnp.zeros((LANES - blocks, nobs), F32)], axis=0).T

    def one_term(b, carry):
        column = jnp.sum(jnp.where(obs_lane == b, low_cols, 0.0), axis=1, keepdims=True)
        terms[pl.ds(b, 1), :] = jnp.sum(weights[b].astype(F32) * column, axis=0, keepdims=True)
        return carry

    lax.fori_loop(0, blocks, one_term, 0)
    outgoing = exact_dot(slot_block.astype(BF16), terms[...])
    for c in range(CAP):
        term_out[:, 0, pl.ds(c * patch_width, patch_width)] = outgoing[c * n_x : (c + 1) * n_x]
    sent_term = send_all(term_out, term_in, 2)
    sent_term.wait()
    returned = jnp.concatenate(
        [term_in[:, 0, pl.ds(c * patch_width, patch_width)] for c in range(CAP)], axis=0
    )

    asked_cols = jnp.concatenate(
        [asked, jnp.full((LANES - slots, LANES), -1.0, F32)], axis=0
    ).T[:rows, :slots]
    cell = row_iota((rows, slots)) * segs
    spread = jnp.concatenate(
        [
            jnp.where(asked_cols == (cell + (level * rows * segs + s)).astype(F32), 1.0, 0.0)
            for level in range(levels)
            for s in range(segs)
        ],
        axis=0,
    ).astype(BF16)
    forcing = exact_dot(spread, returned)
    for level in range(levels):
        for s in range(segs):
            start = (level * segs + s) * rows
            for v in range(VARS):
                plane = v * levels + level
                field_c[plane, s, own, :] = (
                    std[plane, s]
                    * forcing[start : start + rows, v * LANES : (v + 1) * LANES]
                )
    for side, t in ((0, 0), (1, segs - 1)):
        strip = jnp.zeros((rows, LANES), F32)
        for plane in range(planes):
            value = field_c[plane, t, own, :]
            shift = (plane * RIM + side * RIM) % LANES
            if shift:
                value = pltpu.roll(value, shift, 1)
            here = (strip_lane >= plane * RIM) & (strip_lane < (plane + 1) * RIM)
            strip = jnp.where(here, value, strip)
        strip_out2[side] = strip
    sent_x2 = send_x((field_c,), (x2_send, x2_recv))
    sent_y2 = send_y(strip_out2, strip_in2, (y2_send, y2_recv))
    for copy in sent_x2 + sent_y2:
        copy.wait()
    for plane in range(planes):
        field_c[plane, segs, ext, :] = unpack(strip_in2, plane)

    diffuse(field_c, field_b, fx, fy, levels, rows)

    stores = []
    for s in range(segs):
        for plane in range(planes):
            out_tile[plane, s] = (
                xin[plane, s, own, :]
                + sea[plane % levels, s, own, :] * field_c[plane, s, own, :]
            )
        copy = pltpu.make_async_copy(
            out_tile.at[:, s, :, :],
            gradient.at[:, :, pl.ds(s * LANES, LANES)],
            load_sem.at[s],
        )
        copy.start()
        stores.append(copy)
    for copy in stores:
        copy.wait()


def body(
    n_x,
    n_y,
    control,
    background_std,
    kappa_x,
    kappa_y,
    sea_mask,
    obs_weights,
    obs_values,
    obs_rinv,
    obs_tile,
    obs_offset,
):
    planes, rows, cols = control.shape
    levels = kappa_x.shape[0]
    blocks, nobs, width = obs_weights.shape
    segs = cols // LANES
    height = rows + 4 * RIM
    inputs = planes + 2 * levels
    hbm = pl.BlockSpec(memory_space=pl.ANY)
    vmem = pl.BlockSpec(memory_space=pltpu.VMEM)
    dma = pltpu.SemaphoreType.DMA
    field = pltpu.VMEM((planes, segs + 1, height, LANES), F32)
    face = pltpu.VMEM((levels, segs + 1, height, LANES), F32)
    return pl.pallas_call(
        functools.partial(kernel, n_x, n_y),
        out_shape=(
            jax.ShapeDtypeStruct(control.shape, F32),
            jax.ShapeDtypeStruct(obs_values.shape, F32),
        ),
        in_specs=[hbm] * 6 + [vmem] * 4,
        out_specs=(hbm, vmem),
        scratch_shapes=[
            pltpu.VMEM((inputs, segs, height, LANES), F32),
            pltpu.VMEM((levels, segs, height, LANES), jnp.int32),
            pltpu.VMEM((planes, segs, rows, LANES), F32),
            pltpu.VMEM((blocks, nobs, width), BF16),
            face,
            face,
            face,
            field,
            field,
            field,
            pltpu.VMEM((2, rows, LANES), F32),
            pltpu.VMEM((2, height, LANES), F32),
            pltpu.VMEM((2, rows, LANES), F32),
            pltpu.VMEM((2, height, LANES), F32),
            pltpu.VMEM((n_x, 1, CAP * LANES), F32),
            pltpu.VMEM((n_x, 1, CAP * LANES), F32),
            pltpu.VMEM((n_x, 1, CAP * width), F32),
            pltpu.VMEM((n_x, 1, CAP * width), F32),
            pltpu.VMEM((n_x, 1, CAP * width), F32),
            pltpu.VMEM((n_x, 1, CAP * width), F32),
            pltpu.VMEM((blocks, width), F32),
            pltpu.VMEM((planes, segs, rows, LANES), F32),
            dma((5 * segs + 1,)),
            dma((4,)),
            dma((4,)),
            dma((6,)),
            dma((6,)),
            dma((2,)),
            dma((2,)),
            dma((6,)),
            dma((6,)),
            dma((3,)),
            dma((3,)),
        ],
        compiler_params=pltpu.CompilerParams(
            collective_id=0, has_side_effects=True, vmem_limit_bytes=66_000_000
        ),
        name="variational_gradient",
    )(
        control,
        background_std,
        kappa_x,
        kappa_y,
        sea_mask,
        obs_weights,
        obs_values,
        obs_rinv,
        obs_tile.reshape(1, blocks),
        obs_offset.reshape(1, blocks),
    )


def solution(mesh):
    grid = P(None, "gx", "gy")
    holder = ("gx", "gy")
    in_specs = (
        grid,
        grid,
        grid,
        grid,
        grid,
        P(holder, None, None),
        P(holder, None),
        P(holder, None),
        P(holder, None),
        P(holder),
    )
    return jax.shard_map(
        functools.partial(body, mesh.shape["gx"], mesh.shape["gy"]),
        mesh=mesh,
        in_specs=in_specs,
        out_specs=(grid, P(holder, None)),
        check_vma=False,
    )
```

```python
import functools

import jax
import jax.numpy as jnp
from jax import lax
from jax.experimental import pallas as pl
from jax.experimental.pallas import tpu as pltpu
from jax.sharding import PartitionSpec as P

VARS = 2
NSTEP = 8
LANES = 128
RIM = 8
CAP = 2
TOP = 2 * RIM
CHUNK = 16
MESH = pl.DeviceIdType.MESH
F32 = jnp.float32
BF16 = jnp.bfloat16


def lane_iota(shape):
    return lax.broadcasted_iota(jnp.int32, shape, len(shape) - 1)


def row_iota(shape):
    return lax.broadcasted_iota(jnp.int32, shape, len(shape) - 2)


def north_of(tiles, last_lane):
    rolled = [pltpu.roll(tile, LANES - 1, 1) for tile in tiles]
    count = len(tiles)
    return [jnp.where(last_lane, rolled[(t + 1) % count], rolled[t]) for t in range(count)]


def south_of(tiles, first_lane):
    rolled = [pltpu.roll(tile, 1, 1) for tile in tiles]
    count = len(tiles)
    return [jnp.where(first_lane, rolled[(t - 1) % count], rolled[t]) for t in range(count)]


def diffuse(field, spare, fx, fy, levels, rows):
    ntile = field.shape[1]
    first_lane = lane_iota((CHUNK, LANES)) == 0
    last_lane = lane_iota((CHUNK, LANES)) == LANES - 1

    def sweep(src, dst):
        def chunk(number, carry):
            base = RIM + number * CHUNK
            here, above, below = (
                pl.ds(pl.multiple_of(base, 8), CHUNK),
                pl.ds(base + 1, CHUNK),
                pl.ds(base - 1, CHUNK),
            )
            for level in range(levels):
                east = [fx[level, t, here, :] for t in range(ntile)]
                west = [fx[level, t, below, :] for t in range(ntile)]
                north = [fy[level, t, here, :] for t in range(ntile)]
                for var in range(VARS):
                    plane = var * levels + level
                    center = [src[plane, t, here, :] for t in range(ntile)]
                    up = north_of(center, last_lane)
                    flux = [north[t] * (up[t] - center[t]) for t in range(ntile)]
                    back = south_of(flux, first_lane)
                    for t in range(ntile):
                        cell = center[t]
                        dst[plane, t, here, :] = (
                            cell
                            + east[t] * (src[plane, t, above, :] - cell)
                            + west[t] * (src[plane, t, below, :] - cell)
                            + flux[t]
                            - back[t]
                        )
            return carry

        lax.fori_loop(0, (rows + 2 * RIM) // CHUNK, chunk, 0)

    def twice(_, carry):
        sweep(field, spare)
        sweep(spare, field)
        return carry

    lax.fori_loop(0, NSTEP // 2, twice, 0)


def split_three(value):
    high = value.astype(BF16)
    rest = value - high.astype(F32)
    middle = rest.astype(BF16)
    low = (rest - middle.astype(F32)).astype(BF16)
    return high, middle, low


def exact_dot(ones, value):
    width = value.shape[1]
    parts = jnp.concatenate(split_three(value), axis=1)
    sums = jnp.dot(ones, parts, preferred_element_type=F32)
    return sums[:, :width] + sums[:, width : 2 * width] + sums[:, 2 * width :]


def kernel(
    n_x,
    n_y,
    control,
    background_std,
    kappa_x,
    kappa_y,
    sea_mask,
    obs_weights,
    obs_values,
    obs_rinv,
    tile_row,
    offset_row,
    gradient,
    departures,
    xin,
    sea_in,
    std,
    weights,
    sea,
    fx,
    fy,
    field_a,
    field_b,
    field_c,
    strip_out,
    strip_in,
    strip_out2,
    strip_in2,
    index_out,
    index_in,
    patch_out,
    patch_in,
    term_out,
    term_in,
    terms,
    out_tile,
    load_sem,
    x_send,
    x_recv,
    y_send,
    y_recv,
    x2_send,
    x2_recv,
    y2_send,
    y2_recv,
    all_send,
    all_recv,
):
    planes, rows, cols = control.shape
    levels = planes // VARS
    blocks = obs_values.shape[0]
    segs = cols // LANES
    ix, jy = lax.axis_index("gx"), lax.axis_index("gy")
    east, west = lax.rem(ix + 1, n_x), lax.rem(ix + n_x - 1, n_x)
    north, south = lax.rem(jy + 1, n_y), lax.rem(jy + n_y - 1, n_y)
    own = pl.ds(TOP, rows)
    low_rim, high_rim = pl.ds(RIM, RIM), pl.ds(TOP + rows, RIM)
    low_edge, high_edge = pl.ds(TOP, RIM), pl.ds(TOP + rows - RIM, RIM)
    ext = pl.ds(RIM, rows + 2 * RIM)
    ext_rows = rows + 2 * RIM
    height = rows + 4 * RIM

    barrier = pltpu.get_barrier_semaphore()

    def greet(step, carry):
        pl.semaphore_signal(
            barrier, inc=1, device_id=(lax.rem(ix + step, n_x), jy), device_id_type=MESH
        )
        return carry

    lax.fori_loop(1, n_x, greet, 0)
    for other_y in (north, south):
        for other_x in (west, ix, east):
            pl.semaphore_signal(
                barrier, inc=1, device_id=(other_x, other_y), device_id_type=MESH
            )

    loads = []

    def load(source, target):
        copy = pltpu.make_async_copy(source, target, load_sem.at[len(loads)])
        copy.start()
        loads.append(copy)

    for t in range(segs):
        span = pl.ds(t * LANES, LANES)
        load(sea_mask.at[:, :, span], sea_in.at[:, t, own, :])
        load(kappa_x.at[:, :, span], xin.at[pl.ds(planes, levels), t, own, :])
        load(kappa_y.at[:, :, span], xin.at[pl.ds(planes + levels, levels), t, own, :])
        load(control.at[:, :, span], xin.at[pl.ds(0, planes), t, own, :])
    late = len(loads)
    for t in range(segs):
        load(background_std.at[:, :, pl.ds(t * LANES, LANES)], std.at[:, t, :, :])
    load(obs_weights, weights)

    edge = jnp.zeros((RIM, LANES), F32)
    for ref in (field_a, field_b, field_c):
        for plane in range(planes):
            for t in range(segs + 1):
                ref[plane, t, pl.ds(0, RIM), :] = edge
                ref[plane, t, pl.ds(height - RIM, RIM), :] = edge
    for level in range(levels):
        for t in range(segs + 1):
            fx[level, t, pl.ds(0, RIM), :] = edge
            sea[level, t, pl.ds(height - RIM, RIM), :] = edge

    row = tile_row[...].astype(F32)
    pair = (blocks, blocks)
    diagonal = lane_iota(pair) == row_iota(pair)
    col = jnp.sum(jnp.where(diagonal, row, 0.0), axis=1, keepdims=True)
    same = col == row
    rank_col = jnp.max(
        jnp.where(same & (lane_iota(pair) < row_iota(pair)), 1.0, 0.0), axis=1, keepdims=True
    )
    rank_row = jnp.max(
        jnp.where(same & (row_iota(pair) < lane_iota(pair)), 1.0, 0.0), axis=0, keepdims=True
    )
    slots = CAP * n_x
    slot_lane = lane_iota((blocks, slots))
    late_lane = slot_lane >= n_x
    block_slot = jnp.where(
        (jnp.where(late_lane, slot_lane - n_x, slot_lane).astype(F32) == col)
        & (jnp.where(late_lane, 1.0, 0.0) == rank_col),
        1.0,
        0.0,
    ).astype(BF16)
    slot_row = row_iota((slots, blocks))
    late_row = slot_row >= n_x
    slot_block = jnp.where(
        (jnp.where(late_row, slot_row - n_x, slot_row).astype(F32) == row)
        & (jnp.where(late_row, 1.0, 0.0) == rank_row),
        1.0,
        0.0,
    )
    wanted = (
        jnp.sum(slot_block * (offset_row[...].astype(F32) + 1.0), axis=1, keepdims=True) - 1.0
    )
    wanted = jnp.broadcast_to(wanted, (slots, LANES))
    for c in range(CAP):
        index_out[:, 0, pl.ds(c * LANES, LANES)] = wanted[c * n_x : (c + 1) * n_x]

    for copy in loads[:late]:
        copy.wait()
    strip_lane = lane_iota((rows, LANES))
    for side, t in ((0, 0), (1, segs - 1)):
        strip = jnp.zeros((rows, LANES), F32)
        for index in range(planes + 2 * levels):
            level = index % levels
            value = jnp.where(sea_in[level, t, own, :] > 0, xin[index, t, own, :], 0.0)
            shift = (index * RIM + side * RIM) % LANES
            if shift:
                value = pltpu.roll(value, shift, 1)
            here = (strip_lane >= index * RIM) & (strip_lane < (index + 1) * RIM)
            strip = jnp.where(here, value, strip)
        strip_out[side] = strip

    pl.semaphore_wait(barrier, n_x - 1 + 6)

    def send(source, target, sems, number, device):
        copy = pltpu.make_async_remote_copy(
            source,
            target,
            sems[0].at[number],
            sems[1].at[number],
            device_id=device,
            device_id_type=MESH,
        )
        copy.start()
        return copy

    def send_x(refs, sems):
        return [
            send(
                ref.at[:, pl.ds(0, segs), edge_rows, :],
                ref.at[:, pl.ds(0, segs), rim_rows, :],
                sems,
                2 * number + side,
                (other, jy),
            )
            for number, ref in enumerate(refs)
            for side, edge_rows, rim_rows, other in (
                (0, low_edge, high_rim, west),
                (1, high_edge, low_rim, east),
            )
        ]

    def send_y(source, target, sems):
        copies = []
        for side, other_y in ((0, south), (1, north)):
            for number, from_rows, to_rows, other_x in (
                (0, pl.ds(0, rows), own, ix),
                (1, pl.ds(0, RIM), high_rim, west),
                (2, pl.ds(rows - RIM, RIM), low_rim, east),
            ):
                copies.append(
                    send(
                        source.at[side, from_rows, :],
                        target.at[1 - side, to_rows, :],
                        sems,
                        3 * side + number,
                        (other_x, other_y),
                    )
                )
        return copies

    def send_all(source, target, number):
        def one(step, carry):
            other = lax.rem(ix + step, n_x)
            pltpu.make_async_remote_copy(
                source.at[other],
                target.at[ix],
                all_send.at[number],
                all_recv.at[number],
                device_id=(other, jy),
                device_id_type=MESH,
            ).start()
            return carry

        lax.fori_loop(1, n_x, one, 0)
        target[pl.ds(ix, 1)] = source[pl.ds(ix, 1)]
        return pltpu.make_async_remote_copy(
            source.at[pl.ds(0, n_x - 1)],
            target.at[pl.ds(0, n_x - 1)],
            all_send.at[number],
            all_recv.at[number],
            device_id=(east, jy),
            device_id_type=MESH,
        )

    sent_y = send_y(strip_out, strip_in, (y_send, y_recv))
    sent_x = send_x((xin, sea_in), (x_send, x_recv))
    sent_index = send_all(index_out, index_in, 0)

    for copy in sent_x:
        copy.wait()
    for level in range(levels):
        for t in range(segs):
            wet = sea_in[level, t, ext, :] > 0
            sea[level, t, ext, :] = jnp.where(wet, 1.0, 0.0)
            fx[level, t, ext, :] = jnp.where(wet, xin[planes + level, t, ext, :], 0.0)
            fy[level, t, ext, :] = jnp.where(wet, xin[planes + levels + level, t, ext, :], 0.0)
            for var in range(VARS):
                plane = var * levels + level
                field_a[plane, t, ext, :] = jnp.where(wet, xin[plane, t, ext, :], 0.0)
    for copy in sent_y:
        copy.wait()
    ext_lane = lane_iota((ext_rows, LANES))
    from_low = (ext_lane >= LANES - RIM) & (jy > 0)
    from_high = (ext_lane < RIM) & (jy < n_y - 1)

    def unpack(strips, index):
        low = pltpu.roll(strips[0, ext, :], (LANES - RIM - index * RIM) % LANES, 1)
        high = strips[1, ext, :]
        if index:
            high = pltpu.roll(high, LANES - index * RIM, 1)
        return jnp.where(from_high, high, jnp.where(from_low, low, 0.0))

    for plane in range(planes):
        field_a[plane, segs, ext, :] = unpack(strip_in, plane)
    for level in range(levels):
        face = unpack(strip_in, planes + level)
        fx[level, segs, ext, :] = face
        sea[level, segs, ext, :] = jnp.where(face > 0.0, 1.0, 0.0)
        fy[level, segs, ext, :] = unpack(strip_in, planes + levels + level)
    last_lane = ext_lane == LANES - 1
    for level in range(levels):
        wet_north = north_of([sea[level, t, ext, :] for t in range(segs + 1)], last_lane)
        for t in range(segs + 1):
            fx[level, t, ext, :] = (
                fx[level, t, ext, :] * sea[level, t, pl.ds(RIM + 1, ext_rows), :]
            )
            fy[level, t, ext, :] = fy[level, t, ext, :] * wet_north[t]

    diffuse(field_a, field_b, fx, fy, levels, rows)

    for copy in loads[late:]:
        copy.wait()
    sent_index.wait()
    asked = jnp.concatenate(
        [index_in[:, 0, pl.ds(c * LANES, LANES)] for c in range(CAP)], axis=0
    )
    number = lane_iota((slots, LANES)) * segs
    if rows < LANES:
        number = jnp.where(number < rows * segs, number, -2)
    hits = jnp.concatenate(
        [
            jnp.where(asked == (number + (level * rows * segs + s)).astype(F32), 1.0, 0.0)
            for level in range(levels)
            for s in range(segs)
        ],
        axis=1,
    ).astype(BF16)
    table = jnp.concatenate(
        [
            jnp.concatenate(
                [
                    (std[v * levels + level, s] * field_a[v * levels + level, s, own, :]).astype(
                        BF16
                    )
                    for v in range(VARS)
                ],
                axis=1,
            )
            for level in range(levels)
            for s in range(segs)
        ],
        axis=0,
    )
    patch_width = VARS * LANES
    picked = jnp.dot(hits, table, preferred_element_type=F32)
    for c in range(CAP):
        patch_out[:, 0, pl.ds(c * patch_width, patch_width)] = picked[c * n_x : (c + 1) * n_x]
    sent_patch = send_all(patch_out, patch_in, 1)
    sent_patch.wait()
    arrived = jnp.concatenate(
        [patch_in[:, 0, pl.ds(c * patch_width, patch_width)] for c in range(CAP)], axis=0
    ).astype(BF16)
    patches = jnp.dot(block_slot, arrived, preferred_element_type=F32).astype(BF16)

    nobs = obs_values.shape[1]
    obs_lane = lane_iota((nobs, LANES))
    padded = jnp.concatenate(
        [patches, jnp.zeros((LANES - blocks, patch_width), BF16)], axis=0
    )

    def one_equivalent(b, total):
        product = lax.dot_general(
            weights[b], padded, (((1,), (1,)), ((), ())), preferred_element_type=F32
        )
        return jnp.where(obs_lane == b, product, total)

    equivalents = lax.fori_loop(0, blocks, one_equivalent, jnp.zeros((nobs, LANES), F32))
    departed = obs_rinv[...] * (equivalents.T[:blocks] - obs_values[...])
    departures[...] = departed
    low = departed.astype(BF16).astype(F32)
    low_cols = jnp.concatenate([low, jnp.zeros((LANES - blocks, nobs), F32)], axis=0).T

    def one_term(b, carry):
        column = jnp.sum(jnp.where(obs_lane == b, low_cols, 0.0), axis=1, keepdims=True)
        terms[pl.ds(b, 1), :] = jnp.sum(weights[b].astype(F32) * column, axis=0, keepdims=True)
        return carry

    lax.fori_loop(0, blocks, one_term, 0)
    outgoing = exact_dot(slot_block.astype(BF16), terms[...])
    for c in range(CAP):
        term_out[:, 0, pl.ds(c * patch_width, patch_width)] = outgoing[c * n_x : (c + 1) * n_x]
    sent_term = send_all(term_out, term_in, 2)
    sent_term.wait()
    returned = jnp.concatenate(
        [term_in[:, 0, pl.ds(c * patch_width, patch_width)] for c in range(CAP)], axis=0
    )

    asked_cols = jnp.concatenate(
        [asked, jnp.full((LANES - slots, LANES), -1.0, F32)], axis=0
    ).T[:rows, :slots]
    cell = row_iota((rows, slots)) * segs
    spread = jnp.concatenate(
        [
            jnp.where(asked_cols == (cell + (level * rows * segs + s)).astype(F32), 1.0, 0.0)
            for level in range(levels)
            for s in range(segs)
        ],
        axis=0,
    ).astype(BF16)
    forcing = exact_dot(spread, returned)
    for level in range(levels):
        for s in range(segs):
            start = (level * segs + s) * rows
            for v in range(VARS):
                plane = v * levels + level
                field_c[plane, s, own, :] = (
                    std[plane, s]
                    * forcing[start : start + rows, v * LANES : (v + 1) * LANES]
                )
    for side, t in ((0, 0), (1, segs - 1)):
        strip = jnp.zeros((rows, LANES), F32)
        for plane in range(planes):
            value = field_c[plane, t, own, :]
            shift = (plane * RIM + side * RIM) % LANES
            if shift:
                value = pltpu.roll(value, shift, 1)
            here = (strip_lane >= plane * RIM) & (strip_lane < (plane + 1) * RIM)
            strip = jnp.where(here, value, strip)
        strip_out2[side] = strip
    sent_x2 = send_x((field_c,), (x2_send, x2_recv))
    sent_y2 = send_y(strip_out2, strip_in2, (y2_send, y2_recv))
    for copy in sent_x2 + sent_y2:
        copy.wait()
    for plane in range(planes):
        field_c[plane, segs, ext, :] = unpack(strip_in2, plane)

    diffuse(field_c, field_b, fx, fy, levels, rows)

    stores = []
    for s in range(segs):
        for plane in range(planes):
            out_tile[plane, s] = (
                xin[plane, s, own, :]
                + sea[plane % levels, s, own, :] * field_c[plane, s, own, :]
            )
        copy = pltpu.make_async_copy(
            out_tile.at[:, s, :, :],
            gradient.at[:, :, pl.ds(s * LANES, LANES)],
            load_sem.at[s],
        )
        copy.start()
        stores.append(copy)
    for copy in stores:
        copy.wait()


def body(
    n_x,
    n_y,
    control,
    background_std,
    kappa_x,
    kappa_y,
    sea_mask,
    obs_weights,
    obs_values,
    obs_rinv,
    obs_tile,
    obs_offset,
):
    planes, rows, cols = control.shape
    levels = kappa_x.shape[0]
    blocks, nobs, width = obs_weights.shape
    segs = cols // LANES
    height = rows + 4 * RIM
    inputs = planes + 2 * levels
    hbm = pl.BlockSpec(memory_space=pl.ANY)
    vmem = pl.BlockSpec(memory_space=pltpu.VMEM)
    dma = pltpu.SemaphoreType.DMA
    field = pltpu.VMEM((planes, segs + 1, height, LANES), F32)
    face = pltpu.VMEM((levels, segs + 1, height, LANES), F32)
    return pl.pallas_call(
        functools.partial(kernel, n_x, n_y),
        out_shape=(
            jax.ShapeDtypeStruct(control.shape, F32),
            jax.ShapeDtypeStruct(obs_values.shape, F32),
        ),
        in_specs=[hbm] * 6 + [vmem] * 4,
        out_specs=(hbm, vmem),
        scratch_shapes=[
            pltpu.VMEM((inputs, segs, height, LANES), F32),
            pltpu.VMEM((levels, segs, height, LANES), jnp.int32),
            pltpu.VMEM((planes, segs, rows, LANES), F32),
            pltpu.VMEM((blocks, nobs, width), BF16),
            face,
            face,
            face,
            field,
            field,
            field,
            pltpu.VMEM((2, rows, LANES), F32),
            pltpu.VMEM((2, height, LANES), F32),
            pltpu.VMEM((2, rows, LANES), F32),
            pltpu.VMEM((2, height, LANES), F32),
            pltpu.VMEM((n_x, 1, CAP * LANES), F32),
            pltpu.VMEM((n_x, 1, CAP * LANES), F32),
            pltpu.VMEM((n_x, 1, CAP * width), F32),
            pltpu.VMEM((n_x, 1, CAP * width), F32),
            pltpu.VMEM((n_x, 1, CAP * width), F32),
            pltpu.VMEM((n_x, 1, CAP * width), F32),
            pltpu.VMEM((blocks, width), F32),
            pltpu.VMEM((planes, segs, rows, LANES), F32),
            dma((5 * segs + 1,)),
            dma((4,)),
            dma((4,)),
            dma((6,)),
            dma((6,)),
            dma((2,)),
            dma((2,)),
            dma((6,)),
            dma((6,)),
            dma((3,)),
            dma((3,)),
        ],
        compiler_params=pltpu.CompilerParams(
            collective_id=0, has_side_effects=True, vmem_limit_bytes=66_000_000
        ),
        name="variational_gradient",
    )(
        control,
        background_std,
        kappa_x,
        kappa_y,
        sea_mask,
        obs_weights,
        obs_values,
        obs_rinv,
        obs_tile.reshape(1, blocks),
        obs_offset.reshape(1, blocks),
    )


def solution(mesh):
    grid = P(None, "gx", "gy")
    holder = ("gx", "gy")
    in_specs = (
        grid,
        grid,
        grid,
        grid,
        grid,
        P(holder, None, None),
        P(holder, None),
        P(holder, None),
        P(holder, None),
        P(holder),
    )
    return jax.shard_map(
        functools.partial(body, mesh.shape["gx"], mesh.shape["gy"]),
        mesh=mesh,
        in_specs=in_specs,
        out_specs=(grid, P(holder, None)),
        check_vma=False,
    )
```

```python
import functools

import jax
import jax.numpy as jnp
from jax import lax
from jax.experimental import pallas as pl
from jax.experimental.pallas import tpu as pltpu
from jax.sharding import PartitionSpec as P

VARS = 2
NSTEP = 8
LANES = 128
RIM = 8
CAP = 2
TOP = 2 * RIM
GROUP = 8
MESH = pl.DeviceIdType.MESH
F32 = jnp.float32
BF16 = jnp.bfloat16


def lane_iota(shape):
    return lax.broadcasted_iota(jnp.int32, shape, len(shape) - 1)


def row_iota(shape):
    return lax.broadcasted_iota(jnp.int32, shape, len(shape) - 2)


def north_of(tiles, last_lane):
    rolled = [pltpu.roll(tile, LANES - 1, 1) for tile in tiles]
    count = len(tiles)
    return [jnp.where(last_lane, rolled[(t + 1) % count], rolled[t]) for t in range(count)]


def south_of(tiles, first_lane):
    rolled = [pltpu.roll(tile, 1, 1) for tile in tiles]
    count = len(tiles)
    return [jnp.where(first_lane, rolled[(t - 1) % count], rolled[t]) for t in range(count)]


def diffuse(field, spare, fx, fy, levels, rows):
    ntile = field.shape[1]
    count = rows + 2 * RIM
    here, above, below = pl.ds(RIM, count), pl.ds(RIM + 1, count), pl.ds(RIM - 1, count)
    first_lane = lane_iota((count, LANES)) == 0
    last_lane = lane_iota((count, LANES)) == LANES - 1

    def sweep(src, dst):
        for level in range(levels):
            east = [fx[level, t, here, :] for t in range(ntile)]
            west = [fx[level, t, below, :] for t in range(ntile)]
            north = [fy[level, t, here, :] for t in range(ntile)]
            for var in range(VARS):
                plane = var * levels + level
                center = [src[plane, t, here, :] for t in range(ntile)]
                up = north_of(center, last_lane)
                flux = [north[t] * (up[t] - center[t]) for t in range(ntile)]
                back = south_of(flux, first_lane)
                for t in range(ntile):
                    cell = center[t]
                    dst[plane, t, here, :] = (
                        cell
                        + east[t] * (src[plane, t, above, :] - cell)
                        + west[t] * (src[plane, t, below, :] - cell)
                        + flux[t]
                        - back[t]
                    )

    def twice(_, carry):
        sweep(field, spare)
        sweep(spare, field)
        return carry

    lax.fori_loop(0, NSTEP // 2, twice, 0)


def split_three(value):
    high = value.astype(BF16)
    rest = value - high.astype(F32)
    middle = rest.astype(BF16)
    low = (rest - middle.astype(F32)).astype(BF16)
    return high, middle, low


def exact_dot(ones, value):
    width = value.shape[1]
    parts = jnp.concatenate(split_three(value), axis=1)
    sums = jnp.dot(ones, parts, preferred_element_type=F32)
    return sums[:, :width] + sums[:, width : 2 * width] + sums[:, 2 * width :]


def kernel(
    n_x,
    n_y,
    control,
    background_std,
    kappa_x,
    kappa_y,
    sea_mask,
    obs_weights,
    obs_values_in,
    obs_rinv_in,
    tile_row_in,
    offset_row_in,
    gradient,
    departures,
    xin,
    sea_in,
    std,
    weights,
    sea,
    fx,
    fy,
    field_a,
    field_b,
    field_c,
    strip_out,
    strip_in,
    strip_out2,
    strip_in2,
    index_out,
    index_in,
    patch_out,
    patch_in,
    term_out,
    term_in,
    terms,
    out_tile,
    obs_values,
    obs_rinv,
    tile_row,
    offset_row,
    load_sem,
    x_send,
    x_recv,
    y_send,
    y_recv,
    x2_send,
    x2_recv,
    y2_send,
    y2_recv,
    all_send,
    all_recv,
):
    planes, rows, cols = control.shape
    levels = planes // VARS
    blocks = obs_values.shape[0]
    segs = cols // LANES
    ix, jy = lax.axis_index("gx"), lax.axis_index("gy")
    east, west = lax.rem(ix + 1, n_x), lax.rem(ix + n_x - 1, n_x)
    north, south = lax.rem(jy + 1, n_y), lax.rem(jy + n_y - 1, n_y)
    own = pl.ds(TOP, rows)
    low_rim, high_rim = pl.ds(RIM, RIM), pl.ds(TOP + rows, RIM)
    low_edge, high_edge = pl.ds(TOP, RIM), pl.ds(TOP + rows - RIM, RIM)
    ext = pl.ds(RIM, rows + 2 * RIM)
    ext_rows = rows + 2 * RIM
    height = rows + 4 * RIM

    barrier = pltpu.get_barrier_semaphore()

    def greet(step, carry):
        pl.semaphore_signal(
            barrier, inc=1, device_id=(lax.rem(ix + step, n_x), jy), device_id_type=MESH
        )
        return carry

    lax.fori_loop(1, n_x, greet, 0)
    for other_y in (north, south):
        for other_x in (west, ix, east):
            pl.semaphore_signal(
                barrier, inc=1, device_id=(other_x, other_y), device_id_type=MESH
            )

    loads = []

    def load(source, target):
        copy = pltpu.make_async_copy(source, target, load_sem.at[len(loads)])
        copy.start()
        loads.append(copy)

    for t in range(segs):
        span = pl.ds(t * LANES, LANES)
        load(sea_mask.at[:, :, span], sea_in.at[:, t, own, :])
        load(kappa_x.at[:, :, span], xin.at[pl.ds(planes, levels), t, own, :])
        load(kappa_y.at[:, :, span], xin.at[pl.ds(planes + levels, levels), t, own, :])
        load(control.at[:, :, span], xin.at[pl.ds(0, planes), t, own, :])
    late = len(loads)
    load(tile_row_in, tile_row)
    load(offset_row_in, offset_row)
    small = len(loads)
    load(obs_values_in, obs_values)
    load(obs_rinv_in, obs_rinv)
    for t in range(segs):
        load(background_std.at[:, :, pl.ds(t * LANES, LANES)], std.at[:, t, :, :])
    load(obs_weights, weights)

    edge = jnp.zeros((RIM, LANES), F32)
    for ref in (field_a, field_b, field_c):
        for plane in range(planes):
            for t in range(segs + 1):
                ref[plane, t, pl.ds(0, RIM), :] = edge
                ref[plane, t, pl.ds(height - RIM, RIM), :] = edge
    for level in range(levels):
        for t in range(segs + 1):
            fx[level, t, pl.ds(0, RIM), :] = edge
            sea[level, t, pl.ds(height - RIM, RIM), :] = edge

    for copy in loads[late:small]:
        copy.wait()
    row = tile_row[...].astype(F32)
    pair = (blocks, blocks)
    diagonal = lane_iota(pair) == row_iota(pair)
    col = jnp.sum(jnp.where(diagonal, row, 0.0), axis=1, keepdims=True)
    same = col == row
    rank_col = jnp.max(
        jnp.where(same & (lane_iota(pair) < row_iota(pair)), 1.0, 0.0), axis=1, keepdims=True
    )
    rank_row = jnp.max(
        jnp.where(same & (row_iota(pair) < lane_iota(pair)), 1.0, 0.0), axis=0, keepdims=True
    )
    slots = CAP * n_x
    slot_lane = lane_iota((blocks, slots))
    late_lane = slot_lane >= n_x
    block_slot = jnp.where(
        (jnp.where(late_lane, slot_lane - n_x, slot_lane).astype(F32) == col)
        & (jnp.where(late_lane, 1.0, 0.0) == rank_col),
        1.0,
        0.0,
    ).astype(BF16)
    slot_row = row_iota((slots, blocks))
    late_row = slot_row >= n_x
    slot_block = jnp.where(
        (jnp.where(late_row, slot_row - n_x, slot_row).astype(F32) == row)
        & (jnp.where(late_row, 1.0, 0.0) == rank_row),
        1.0,
        0.0,
    )
    wanted = (
        jnp.sum(slot_block * (offset_row[...].astype(F32) + 1.0), axis=1, keepdims=True) - 1.0
    )
    wanted = jnp.broadcast_to(wanted, (slots, LANES))
    for c in range(CAP):
        index_out[:, 0, pl.ds(c * LANES, LANES)] = wanted[c * n_x : (c + 1) * n_x]

    for copy in loads[:late]:
        copy.wait()
    strip_lane = lane_iota((rows, LANES))
    for side, t in ((0, 0), (1, segs - 1)):
        strip = jnp.zeros((rows, LANES), F32)
        for index in range(planes + 2 * levels):
            level = index % levels
            value = jnp.where(sea_in[level, t, own, :] > 0, xin[index, t, own, :], 0.0)
            shift = (index * RIM + side * RIM) % LANES
            if shift:
                value = pltpu.roll(value, shift, 1)
            here = (strip_lane >= index * RIM) & (strip_lane < (index + 1) * RIM)
            strip = jnp.where(here, value, strip)
        strip_out[side] = strip

    pl.semaphore_wait(barrier, n_x - 1 + 6)

    def send(source, target, sems, number, device):
        copy = pltpu.make_async_remote_copy(
            source,
            target,
            sems[0].at[number],
            sems[1].at[number],
            device_id=device,
            device_id_type=MESH,
        )
        copy.start()
        return copy

    def send_x(refs, sems):
        return [
            send(
                ref.at[:, pl.ds(0, segs), edge_rows, :],
                ref.at[:, pl.ds(0, segs), rim_rows, :],
                sems,
                2 * number + side,
                (other, jy),
            )
            for number, ref in enumerate(refs)
            for side, edge_rows, rim_rows, other in (
                (0, low_edge, high_rim, west),
                (1, high_edge, low_rim, east),
            )
        ]

    def send_y(source, target, sems):
        copies = []
        for side, other_y in ((0, south), (1, north)):
            for number, from_rows, to_rows, other_x in (
                (0, pl.ds(0, rows), own, ix),
                (1, pl.ds(0, RIM), high_rim, west),
                (2, pl.ds(rows - RIM, RIM), low_rim, east),
            ):
                copies.append(
                    send(
                        source.at[side, from_rows, :],
                        target.at[1 - side, to_rows, :],
                        sems,
                        3 * side + number,
                        (other_x, other_y),
                    )
                )
        return copies

    def send_all(source, target, number):
        def one(step, carry):
            other = lax.rem(ix + step, n_x)
            pltpu.make_async_remote_copy(
                source.at[other],
                target.at[ix],
                all_send.at[number],
                all_recv.at[number],
                device_id=(other, jy),
                device_id_type=MESH,
            ).start()
            return carry

        lax.fori_loop(1, n_x, one, 0)
        target[pl.ds(ix, 1)] = source[pl.ds(ix, 1)]
        return pltpu.make_async_remote_copy(
            source.at[pl.ds(0, n_x - 1)],
            target.at[pl.ds(0, n_x - 1)],
            all_send.at[number],
            all_recv.at[number],
            device_id=(east, jy),
            device_id_type=MESH,
        )

    sent_y = send_y(strip_out, strip_in, (y_send, y_recv))
    sent_x = send_x((xin, sea_in), (x_send, x_recv))
    sent_index = send_all(index_out, index_in, 0)

    for copy in sent_x:
        copy.wait()
    for level in range(levels):
        for t in range(segs):
            wet = sea_in[level, t, ext, :] > 0
            sea[level, t, ext, :] = jnp.where(wet, 1.0, 0.0)
            fx[level, t, ext, :] = jnp.where(wet, xin[planes + level, t, ext, :], 0.0)
            fy[level, t, ext, :] = jnp.where(wet, xin[planes + levels + level, t, ext, :], 0.0)
            for var in range(VARS):
                plane = var * levels + level
                field_a[plane, t, ext, :] = jnp.where(wet, xin[plane, t, ext, :], 0.0)
    for copy in sent_y:
        copy.wait()
    ext_lane = lane_iota((ext_rows, LANES))
    from_low = (ext_lane >= LANES - RIM) & (jy > 0)
    from_high = (ext_lane < RIM) & (jy < n_y - 1)

    def unpack(strips, index):
        low = pltpu.roll(strips[0, ext, :], (LANES - RIM - index * RIM) % LANES, 1)
        high = strips[1, ext, :]
        if index:
            high = pltpu.roll(high, LANES - index * RIM, 1)
        return jnp.where(from_high, high, jnp.where(from_low, low, 0.0))

    for plane in range(planes):
        field_a[plane, segs, ext, :] = unpack(strip_in, plane)
    for level in range(levels):
        face = unpack(strip_in, planes + level)
        fx[level, segs, ext, :] = face
        sea[level, segs, ext, :] = jnp.where(face > 0.0, 1.0, 0.0)
        fy[level, segs, ext, :] = unpack(strip_in, planes + levels + level)
    last_lane = ext_lane == LANES - 1
    for level in range(levels):
        wet_north = north_of([sea[level, t, ext, :] for t in range(segs + 1)], last_lane)
        for t in range(segs + 1):
            fx[level, t, ext, :] = (
                fx[level, t, ext, :] * sea[level, t, pl.ds(RIM + 1, ext_rows), :]
            )
            fy[level, t, ext, :] = fy[level, t, ext, :] * wet_north[t]

    diffuse(field_a, field_b, fx, fy, levels, rows)

    for copy in loads[small:]:
        copy.wait()
    sent_index.wait()
    asked = jnp.concatenate(
        [index_in[:, 0, pl.ds(c * LANES, LANES)] for c in range(CAP)], axis=0
    )
    number = lane_iota((slots, LANES)) * segs
    if rows < LANES:
        number = jnp.where(number < rows * segs, number, -2)
    hits = jnp.concatenate(
        [
            jnp.where(asked == (number + (level * rows * segs + s)).astype(F32), 1.0, 0.0)
            for level in range(levels)
            for s in range(segs)
        ],
        axis=1,
    ).astype(BF16)
    table = jnp.concatenate(
        [
            jnp.concatenate(
                [
                    (std[v * levels + level, s] * field_a[v * levels + level, s, own, :]).astype(
                        BF16
                    )
                    for v in range(VARS)
                ],
                axis=1,
            )
            for level in range(levels)
            for s in range(segs)
        ],
        axis=0,
    )
    patch_width = VARS * LANES
    picked = jnp.dot(hits, table, preferred_element_type=F32)
    for c in range(CAP):
        patch_out[:, 0, pl.ds(c * patch_width, patch_width)] = picked[c * n_x : (c + 1) * n_x]
    sent_patch = send_all(patch_out, patch_in, 1)
    sent_patch.wait()
    arrived = jnp.concatenate(
        [patch_in[:, 0, pl.ds(c * patch_width, patch_width)] for c in range(CAP)], axis=0
    ).astype(BF16)
    patches = jnp.dot(block_slot, arrived, preferred_element_type=F32).astype(BF16)

    nobs = obs_values.shape[1]
    obs_lane = lane_iota((nobs, LANES))
    padded = jnp.concatenate(
        [patches, jnp.zeros((LANES - blocks, patch_width), BF16)], axis=0
    )

    def some_equivalents(group, total):
        first = group * GROUP
        product = lax.dot_general(
            weights[pl.ds(first, GROUP)].reshape(GROUP * nobs, patch_width),
            padded,
            (((1,), (1,)), ((), ())),
            preferred_element_type=F32,
        )
        for number in range(GROUP):
            total = jnp.where(
                obs_lane == first + number, product[number * nobs : (number + 1) * nobs], total
            )
        return total

    equivalents = lax.fori_loop(
        0, blocks // GROUP, some_equivalents, jnp.zeros((nobs, LANES), F32)
    )
    departed = obs_rinv[...] * (equivalents.T[:blocks] - obs_values[...])
    departures[...] = departed
    low = departed.astype(BF16).astype(F32)
    low_cols = jnp.concatenate([low, jnp.zeros((LANES - blocks, nobs), F32)], axis=0).T

    def some_terms(group, carry):
        first = group * GROUP
        columns = [
            jnp.sum(jnp.where(obs_lane == first + number, low_cols, 0.0), axis=1, keepdims=True)
            for number in range(GROUP)
        ]
        terms[pl.ds(pl.multiple_of(first, GROUP), GROUP), :] = jnp.concatenate(
            [
                jnp.sum(
                    weights[first + number].astype(F32) * columns[number], axis=0, keepdims=True
                )
                for number in range(GROUP)
            ],
            axis=0,
        )
        return carry

    lax.fori_loop(0, blocks // GROUP, some_terms, 0)
    outgoing = exact_dot(slot_block.astype(BF16), terms[...])
    for c in range(CAP):
        term_out[:, 0, pl.ds(c * patch_width, patch_width)] = outgoing[c * n_x : (c + 1) * n_x]
    sent_term = send_all(term_out, term_in, 2)
    sent_term.wait()
    returned = jnp.concatenate(
        [term_in[:, 0, pl.ds(c * patch_width, patch_width)] for c in range(CAP)], axis=0
    )

    asked_cols = jnp.concatenate(
        [asked, jnp.full((LANES - slots, LANES), -1.0, F32)], axis=0
    ).T[:rows, :slots]
    cell = row_iota((rows, slots)) * segs
    spread = jnp.concatenate(
        [
            jnp.where(asked_cols == (cell + (level * rows * segs + s)).astype(F32), 1.0, 0.0)
            for level in range(levels)
            for s in range(segs)
        ],
        axis=0,
    ).astype(BF16)
    forcing = exact_dot(spread, returned)
    for level in range(levels):
        for s in range(segs):
            start = (level * segs + s) * rows
            for v in range(VARS):
                plane = v * levels + level
                field_c[plane, s, own, :] = (
                    std[plane, s]
                    * forcing[start : start + rows, v * LANES : (v + 1) * LANES]
                )
    sent_x2 = send_x((field_c,), (x2_send, x2_recv))
    for side, t in ((0, 0), (1, segs - 1)):
        strip = jnp.zeros((rows, LANES), F32)
        for plane in range(planes):
            value = field_c[plane, t, own, :]
            shift = (plane * RIM + side * RIM) % LANES
            if shift:
                value = pltpu.roll(value, shift, 1)
            here = (strip_lane >= plane * RIM) & (strip_lane < (plane + 1) * RIM)
            strip = jnp.where(here, value, strip)
        strip_out2[side] = strip
    sent_y2 = send_y(strip_out2, strip_in2, (y2_send, y2_recv))
    for copy in sent_x2 + sent_y2:
        copy.wait()
    for plane in range(planes):
        field_c[plane, segs, ext, :] = unpack(strip_in2, plane)

    diffuse(field_c, field_b, fx, fy, levels, rows)

    stores = []
    for s in range(segs):
        for plane in range(planes):
            out_tile[plane, s] = sea[plane % levels, s, own, :] * field_c[plane, s, own, :]
        copy = pltpu.make_async_copy(
            out_tile.at[:, s, :, :],
            gradient.at[:, :, pl.ds(s * LANES, LANES)],
            load_sem.at[s],
        )
        copy.start()
        stores.append(copy)
    for copy in stores:
        copy.wait()


def finish(increment, control, departed, gradient, departures):
    gradient[...] = control[...] + increment[...]
    departures[...] = departed[...]


def body(
    n_x,
    n_y,
    control,
    background_std,
    kappa_x,
    kappa_y,
    sea_mask,
    obs_weights,
    obs_values,
    obs_rinv,
    obs_tile,
    obs_offset,
):
    planes, rows, cols = control.shape
    levels = kappa_x.shape[0]
    blocks, nobs, width = obs_weights.shape
    segs = cols // LANES
    height = rows + 4 * RIM
    inputs = planes + 2 * levels
    hbm = pl.BlockSpec(memory_space=pl.ANY)
    vmem = pl.BlockSpec(memory_space=pltpu.VMEM)
    dma = pltpu.SemaphoreType.DMA
    field = pltpu.VMEM((planes, segs + 1, height, LANES), F32)
    face = pltpu.VMEM((levels, segs + 1, height, LANES), F32)
    increment, departed = pl.pallas_call(
        functools.partial(kernel, n_x, n_y),
        out_shape=(
            jax.ShapeDtypeStruct(control.shape, F32),
            jax.ShapeDtypeStruct(obs_values.shape, F32),
        ),
        in_specs=[hbm] * 10,
        out_specs=(hbm, vmem),
        scratch_shapes=[
            pltpu.VMEM((inputs, segs, height, LANES), F32),
            pltpu.VMEM((levels, segs, height, LANES), jnp.int32),
            pltpu.VMEM((planes, segs, rows, LANES), F32),
            pltpu.VMEM((blocks, nobs, width), BF16),
            face,
            face,
            face,
            field,
            field,
            field,
            pltpu.VMEM((2, rows, LANES), F32),
            pltpu.VMEM((2, height, LANES), F32),
            pltpu.VMEM((2, rows, LANES), F32),
            pltpu.VMEM((2, height, LANES), F32),
            pltpu.VMEM((n_x, 1, CAP * LANES), F32),
            pltpu.VMEM((n_x, 1, CAP * LANES), F32),
            pltpu.VMEM((n_x, 1, CAP * width), F32),
            pltpu.VMEM((n_x, 1, CAP * width), F32),
            pltpu.VMEM((n_x, 1, CAP * width), F32),
            pltpu.VMEM((n_x, 1, CAP * width), F32),
            pltpu.VMEM((blocks, width), F32),
            pltpu.VMEM((planes, segs, rows, LANES), F32),
            pltpu.VMEM((blocks, nobs), F32),
            pltpu.VMEM((blocks, nobs), F32),
            pltpu.VMEM((1, blocks), jnp.int32),
            pltpu.VMEM((1, blocks), jnp.int32),
            dma((5 * segs + 5,)),
            dma((4,)),
            dma((4,)),
            dma((6,)),
            dma((6,)),
            dma((2,)),
            dma((2,)),
            dma((6,)),
            dma((6,)),
            dma((3,)),
            dma((3,)),
        ],
        compiler_params=pltpu.CompilerParams(
            collective_id=0, has_side_effects=True, vmem_limit_bytes=66_000_000
        ),
        name="variational_gradient",
    )(
        control,
        background_std,
        kappa_x,
        kappa_y,
        sea_mask,
        obs_weights,
        obs_values,
        obs_rinv,
        obs_tile.reshape(1, blocks),
        obs_offset.reshape(1, blocks),
    )
    slab = pl.BlockSpec((1, rows, cols), lambda plane: (plane, 0, 0))
    whole = pl.BlockSpec((blocks, nobs), lambda plane: (0, 0))
    return pl.pallas_call(
        finish,
        grid=(planes,),
        out_shape=(
            jax.ShapeDtypeStruct(control.shape, F32),
            jax.ShapeDtypeStruct(obs_values.shape, F32),
        ),
        in_specs=[slab, slab, whole],
        out_specs=(slab, whole),
        name="add_control",
    )(increment, control, departed)


def solution(mesh):
    grid = P(None, "gx", "gy")
    holder = ("gx", "gy")
    in_specs = (
        grid,
        grid,
        grid,
        grid,
        grid,
        P(holder, None, None),
        P(holder, None),
        P(holder, None),
        P(holder, None),
        P(holder),
    )
    return jax.shard_map(
        functools.partial(body, mesh.shape["gx"], mesh.shape["gy"]),
        mesh=mesh,
        in_specs=in_specs,
        out_specs=(grid, P(holder, None)),
        check_vma=False,
    )
```

```python
import functools

import jax
import jax.numpy as jnp
from jax import lax
from jax.experimental import pallas as pl
from jax.experimental.pallas import tpu as pltpu
from jax.sharding import PartitionSpec as P

VARS = 2
NSTEP = 8
LANES = 128
RIM = 8
CAP = 2
TOP = 2 * RIM
GROUP = 8
CHUNK = 48
MESH = pl.DeviceIdType.MESH
F32 = jnp.float32
BF16 = jnp.bfloat16


def lane_iota(shape):
    return lax.broadcasted_iota(jnp.int32, shape, len(shape) - 1)


def row_iota(shape):
    return lax.broadcasted_iota(jnp.int32, shape, len(shape) - 2)


def north_of(tiles, last_lane):
    rolled = [pltpu.roll(tile, LANES - 1, 1) for tile in tiles]
    count = len(tiles)
    return [jnp.where(last_lane, rolled[(t + 1) % count], rolled[t]) for t in range(count)]


def south_of(tiles, first_lane):
    rolled = [pltpu.roll(tile, 1, 1) for tile in tiles]
    count = len(tiles)
    return [jnp.where(first_lane, rolled[(t - 1) % count], rolled[t]) for t in range(count)]


def to_lanes(nat, target, planes):
    depth, height, _ = target.shape
    run = height // depth
    size = height - 2 * TOP
    low_lane = lane_iota((RIM, LANES)) < LANES // 2
    for step in range(depth):
        pick = pl.ds(step, run, stride=depth)
        own = jnp.concatenate(
            [nat[plane, tile, pick, :] for tile in range(2) for plane in planes], axis=0
        ).T
        rim = jnp.concatenate([nat[plane, 2, pick, :] for plane in planes] * 2, axis=0).T
        target[step, pl.ds(TOP, size), :] = own
        target[step, pl.ds(RIM, RIM), :] = jnp.where(
            low_lane, rim[size - RIM :], pltpu.roll(own[size - RIM :], LANES // 2, 1)
        )
        target[step, pl.ds(TOP + size, RIM), :] = jnp.where(
            low_lane, pltpu.roll(own[:RIM], LANES // 2, 1), rim[:RIM]
        )


def from_lanes(source, nat, planes):
    depth, height, _ = source.shape
    run = height // depth
    for step in range(depth):
        pick = pl.ds(step, run, stride=depth)
        rows = source[step, pl.ds(TOP, height - 2 * TOP), :].T
        for tile in range(2):
            for plane in range(planes):
                start = (tile * planes + plane) * run
                nat[plane, tile, pick, :] = rows[start : start + run]


def diffuse(field, spare, fx, fy):
    depth, height, _ = field.shape

    def sweep(src, dst):
        for base in range(RIM, height - RIM, CHUNK):
            here, above, below = pl.ds(base, CHUNK), pl.ds(base + 1, CHUNK), pl.ds(base - 1, CHUNK)
            wrapped = pltpu.roll(src[0, here, :], LANES - 1, 1)
            back = None
            for step in range(depth):
                cell = src[step, here, :]
                east = src[step + 1, here, :] if step < depth - 1 else wrapped
                flux = fx[step, here, :] * (east - cell)
                total = (
                    cell
                    + flux
                    + fy[step, here, :] * (src[step, above, :] - cell)
                    + fy[step, below, :] * (src[step, below, :] - cell)
                )
                if step:
                    dst[step, here, :] = total - back
                else:
                    dst[0, here, :] = total
                back = flux
            dst[0, here, :] = dst[0, here, :] - pltpu.roll(back, 1, 1)

    def twice(_, carry):
        sweep(field, spare)
        sweep(spare, field)
        return carry

    lax.fori_loop(0, NSTEP // 2, twice, 0)


def split_three(value):
    high = value.astype(BF16)
    rest = value - high.astype(F32)
    middle = rest.astype(BF16)
    low = (rest - middle.astype(F32)).astype(BF16)
    return high, middle, low


def exact_dot(ones, value):
    width = value.shape[1]
    parts = jnp.concatenate(split_three(value), axis=1)
    sums = jnp.dot(ones, parts, preferred_element_type=F32)
    return sums[:, :width] + sums[:, width : 2 * width] + sums[:, 2 * width :]


def kernel(
    n_x,
    n_y,
    control,
    background_std,
    kappa_x,
    kappa_y,
    sea_mask,
    obs_weights,
    obs_values_in,
    obs_rinv_in,
    tile_row_in,
    offset_row_in,
    gradient,
    departures,
    xin,
    sea_in,
    std,
    weights,
    sea,
    fx,
    fy,
    field_a,
    field_c,
    lane_a,
    lane_b,
    lane_x,
    lane_y,
    strip_out,
    strip_in,
    strip_out2,
    strip_in2,
    index_out,
    index_in,
    patch_out,
    patch_in,
    term_out,
    term_in,
    terms,
    out_tile,
    obs_values,
    obs_rinv,
    tile_row,
    offset_row,
    load_sem,
    x_send,
    x_recv,
    y_send,
    y_recv,
    x2_send,
    x2_recv,
    y2_send,
    y2_recv,
    all_send,
    all_recv,
):
    planes, rows, cols = control.shape
    levels = planes // VARS
    blocks = obs_values.shape[0]
    segs = cols // LANES
    ix, jy = lax.axis_index("gx"), lax.axis_index("gy")
    east, west = lax.rem(ix + 1, n_x), lax.rem(ix + n_x - 1, n_x)
    north, south = lax.rem(jy + 1, n_y), lax.rem(jy + n_y - 1, n_y)
    own = pl.ds(TOP, rows)
    low_rim, high_rim = pl.ds(RIM, RIM), pl.ds(TOP + rows, RIM)
    low_edge, high_edge = pl.ds(TOP, RIM), pl.ds(TOP + rows - RIM, RIM)
    ext = pl.ds(RIM, rows + 2 * RIM)
    ext_rows = rows + 2 * RIM
    height = rows + 4 * RIM

    barrier = pltpu.get_barrier_semaphore()

    def greet(step, carry):
        pl.semaphore_signal(
            barrier, inc=1, device_id=(lax.rem(ix + step, n_x), jy), device_id_type=MESH
        )
        return carry

    lax.fori_loop(1, n_x, greet, 0)
    for other_y in (north, south):
        for other_x in (west, ix, east):
            pl.semaphore_signal(
                barrier, inc=1, device_id=(other_x, other_y), device_id_type=MESH
            )

    loads = []

    def load(source, target):
        copy = pltpu.make_async_copy(source, target, load_sem.at[len(loads)])
        copy.start()
        loads.append(copy)

    for t in range(segs):
        span = pl.ds(t * LANES, LANES)
        load(sea_mask.at[:, :, span], sea_in.at[:, t, own, :])
        load(kappa_x.at[:, :, span], xin.at[pl.ds(planes, levels), t, own, :])
        load(kappa_y.at[:, :, span], xin.at[pl.ds(planes + levels, levels), t, own, :])
        load(control.at[:, :, span], xin.at[pl.ds(0, planes), t, own, :])
    late = len(loads)
    load(tile_row_in, tile_row)
    load(offset_row_in, offset_row)
    small = len(loads)
    load(obs_values_in, obs_values)
    load(obs_rinv_in, obs_rinv)
    for t in range(segs):
        load(background_std.at[:, :, pl.ds(t * LANES, LANES)], std.at[:, t, :, :])
    load(obs_weights, weights)

    edge = jnp.zeros((RIM, LANES), F32)
    for ref in (field_a, field_c):
        for plane in range(planes):
            for t in range(segs + 1):
                ref[plane, t, pl.ds(0, RIM), :] = edge
                ref[plane, t, pl.ds(height - RIM, RIM), :] = edge
    for level in range(levels):
        for t in range(segs + 1):
            for ref in (fx, fy):
                ref[level, t, pl.ds(0, RIM), :] = edge
                ref[level, t, pl.ds(height - RIM, RIM), :] = edge
            sea[level, t, pl.ds(height - RIM, RIM), :] = edge

    for ref in (lane_a, lane_b, lane_x, lane_y):
        for step in range(lane_a.shape[0]):
            ref[step, pl.ds(0, RIM), :] = edge
            ref[step, pl.ds(height - RIM, RIM), :] = edge

    for copy in loads[late:small]:
        copy.wait()
    row = tile_row[...].astype(F32)
    pair = (blocks, blocks)
    diagonal = lane_iota(pair) == row_iota(pair)
    col = jnp.sum(jnp.where(diagonal, row, 0.0), axis=1, keepdims=True)
    same = col == row
    rank_col = jnp.max(
        jnp.where(same & (lane_iota(pair) < row_iota(pair)), 1.0, 0.0), axis=1, keepdims=True
    )
    rank_row = jnp.max(
        jnp.where(same & (row_iota(pair) < lane_iota(pair)), 1.0, 0.0), axis=0, keepdims=True
    )
    slots = CAP * n_x
    slot_lane = lane_iota((blocks, slots))
    late_lane = slot_lane >= n_x
    block_slot = jnp.where(
        (jnp.where(late_lane, slot_lane - n_x, slot_lane).astype(F32) == col)
        & (jnp.where(late_lane, 1.0, 0.0) == rank_col),
        1.0,
        0.0,
    ).astype(BF16)
    slot_row = row_iota((slots, blocks))
    late_row = slot_row >= n_x
    slot_block = jnp.where(
        (jnp.where(late_row, slot_row - n_x, slot_row).astype(F32) == row)
        & (jnp.where(late_row, 1.0, 0.0) == rank_row),
        1.0,
        0.0,
    )
    wanted = (
        jnp.sum(slot_block * (offset_row[...].astype(F32) + 1.0), axis=1, keepdims=True) - 1.0
    )
    wanted = jnp.broadcast_to(wanted, (slots, LANES))
    for c in range(CAP):
        index_out[:, 0, pl.ds(c * LANES, LANES)] = wanted[c * n_x : (c + 1) * n_x]

    for copy in loads[:late]:
        copy.wait()
    strip_lane = lane_iota((rows, LANES))
    for side, t in ((0, 0), (1, segs - 1)):
        strip = jnp.zeros((rows, LANES), F32)
        for index in range(planes + 2 * levels):
            level = index % levels
            value = jnp.where(sea_in[level, t, own, :] > 0, xin[index, t, own, :], 0.0)
            shift = (index * RIM + side * RIM) % LANES
            if shift:
                value = pltpu.roll(value, shift, 1)
            here = (strip_lane >= index * RIM) & (strip_lane < (index + 1) * RIM)
            strip = jnp.where(here, value, strip)
        strip_out[side] = strip

    pl.semaphore_wait(barrier, n_x - 1 + 6)

    def send(source, target, sems, number, device):
        copy = pltpu.make_async_remote_copy(
            source,
            target,
            sems[0].at[number],
            sems[1].at[number],
            device_id=device,
            device_id_type=MESH,
        )
        copy.start()
        return copy

    def send_x(refs, sems):
        return [
            send(
                ref.at[:, pl.ds(0, segs), edge_rows, :],
                ref.at[:, pl.ds(0, segs), rim_rows, :],
                sems,
                2 * number + side,
                (other, jy),
            )
            for number, ref in enumerate(refs)
            for side, edge_rows, rim_rows, other in (
                (0, low_edge, high_rim, west),
                (1, high_edge, low_rim, east),
            )
        ]

    def send_y(source, target, sems):
        copies = []
        for side, other_y in ((0, south), (1, north)):
            for number, from_rows, to_rows, other_x in (
                (0, pl.ds(0, rows), own, ix),
                (1, pl.ds(0, RIM), high_rim, west),
                (2, pl.ds(rows - RIM, RIM), low_rim, east),
            ):
                copies.append(
                    send(
                        source.at[side, from_rows, :],
                        target.at[1 - side, to_rows, :],
                        sems,
                        3 * side + number,
                        (other_x, other_y),
                    )
                )
        return copies

    def send_all(source, target, number):
        def one(step, carry):
            other = lax.rem(ix + step, n_x)
            pltpu.make_async_remote_copy(
                source.at[other],
                target.at[ix],
                all_send.at[number],
                all_recv.at[number],
                device_id=(other, jy),
                device_id_type=MESH,
            ).start()
            return carry

        lax.fori_loop(1, n_x, one, 0)
        target[pl.ds(ix, 1)] = source[pl.ds(ix, 1)]
        return pltpu.make_async_remote_copy(
            source.at[pl.ds(0, n_x - 1)],
            target.at[pl.ds(0, n_x - 1)],
            all_send.at[number],
            all_recv.at[number],
            device_id=(east, jy),
            device_id_type=MESH,
        )

    sent_y = send_y(strip_out, strip_in, (y_send, y_recv))
    sent_x = send_x((xin, sea_in), (x_send, x_recv))
    sent_index = send_all(index_out, index_in, 0)

    for copy in sent_x:
        copy.wait()
    for level in range(levels):
        for t in range(segs):
            wet = sea_in[level, t, ext, :] > 0
            sea[level, t, ext, :] = jnp.where(wet, 1.0, 0.0)
            fx[level, t, ext, :] = jnp.where(wet, xin[planes + level, t, ext, :], 0.0)
            fy[level, t, ext, :] = jnp.where(wet, xin[planes + levels + level, t, ext, :], 0.0)
            for var in range(VARS):
                plane = var * levels + level
                field_a[plane, t, ext, :] = jnp.where(wet, xin[plane, t, ext, :], 0.0)
    for copy in sent_y:
        copy.wait()
    ext_lane = lane_iota((ext_rows, LANES))
    from_low = (ext_lane >= LANES - RIM) & (jy > 0)
    from_high = (ext_lane < RIM) & (jy < n_y - 1)

    def unpack(strips, index):
        low = pltpu.roll(strips[0, ext, :], (LANES - RIM - index * RIM) % LANES, 1)
        high = strips[1, ext, :]
        if index:
            high = pltpu.roll(high, LANES - index * RIM, 1)
        return jnp.where(from_high, high, jnp.where(from_low, low, 0.0))

    for plane in range(planes):
        field_a[plane, segs, ext, :] = unpack(strip_in, plane)
    for level in range(levels):
        face = unpack(strip_in, planes + level)
        fx[level, segs, ext, :] = face
        sea[level, segs, ext, :] = jnp.where(face > 0.0, 1.0, 0.0)
        fy[level, segs, ext, :] = unpack(strip_in, planes + levels + level)
    last_lane = ext_lane == LANES - 1
    for level in range(levels):
        wet_north = north_of([sea[level, t, ext, :] for t in range(segs + 1)], last_lane)
        for t in range(segs + 1):
            fx[level, t, ext, :] = (
                fx[level, t, ext, :] * sea[level, t, pl.ds(RIM + 1, ext_rows), :]
            )
            fy[level, t, ext, :] = fy[level, t, ext, :] * wet_north[t]

    faces = list(range(levels)) * VARS
    to_lanes(field_a, lane_a, range(planes))
    to_lanes(fx, lane_x, faces)
    to_lanes(fy, lane_y, faces)
    diffuse(lane_a, lane_b, lane_x, lane_y)
    from_lanes(lane_a, field_a, planes)

    for copy in loads[small:]:
        copy.wait()
    sent_index.wait()
    asked = jnp.concatenate(
        [index_in[:, 0, pl.ds(c * LANES, LANES)] for c in range(CAP)], axis=0
    )
    number = lane_iota((slots, LANES)) * segs
    if rows < LANES:
        number = jnp.where(number < rows * segs, number, -2)
    hits = jnp.concatenate(
        [
            jnp.where(asked == (number + (level * rows * segs + s)).astype(F32), 1.0, 0.0)
            for level in range(levels)
            for s in range(segs)
        ],
        axis=1,
    ).astype(BF16)
    table = jnp.concatenate(
        [
            jnp.concatenate(
                [
                    (std[v * levels + level, s] * field_a[v * levels + level, s, own, :]).astype(
                        BF16
                    )
                    for v in range(VARS)
                ],
                axis=1,
            )
            for level in range(levels)
            for s in range(segs)
        ],
        axis=0,
    )
    patch_width = VARS * LANES
    picked = jnp.dot(hits, table, preferred_element_type=F32)
    for c in range(CAP):
        patch_out[:, 0, pl.ds(c * patch_width, patch_width)] = picked[c * n_x : (c + 1) * n_x]
    sent_patch = send_all(patch_out, patch_in, 1)
    sent_patch.wait()
    arrived = jnp.concatenate(
        [patch_in[:, 0, pl.ds(c * patch_width, patch_width)] for c in range(CAP)], axis=0
    ).astype(BF16)
    patches = jnp.dot(block_slot, arrived, preferred_element_type=F32).astype(BF16)

    nobs = obs_values.shape[1]
    obs_lane = lane_iota((nobs, LANES))
    padded = jnp.concatenate(
        [patches, jnp.zeros((LANES - blocks, patch_width), BF16)], axis=0
    )

    def some_equivalents(group, total):
        first = group * GROUP
        product = lax.dot_general(
            weights[pl.ds(first, GROUP)].reshape(GROUP * nobs, patch_width),
            padded,
            (((1,), (1,)), ((), ())),
            preferred_element_type=F32,
        )
        for number in range(GROUP):
            total = jnp.where(
                obs_lane == first + number, product[number * nobs : (number + 1) * nobs], total
            )
        return total

    equivalents = lax.fori_loop(
        0, blocks // GROUP, some_equivalents, jnp.zeros((nobs, LANES), F32)
    )
    departed = obs_rinv[...] * (equivalents.T[:blocks] - obs_values[...])
    departures[...] = departed
    low = departed.astype(BF16).astype(F32)
    low_cols = jnp.concatenate([low, jnp.zeros((LANES - blocks, nobs), F32)], axis=0).T

    def some_terms(group, carry):
        first = group * GROUP
        columns = [
            jnp.sum(jnp.where(obs_lane == first + number, low_cols, 0.0), axis=1, keepdims=True)
            for number in range(GROUP)
        ]
        terms[pl.ds(pl.multiple_of(first, GROUP), GROUP), :] = jnp.concatenate(
            [
                jnp.sum(
                    weights[first + number].astype(F32) * columns[number], axis=0, keepdims=True
                )
                for number in range(GROUP)
            ],
            axis=0,
        )
        return carry

    lax.fori_loop(0, blocks // GROUP, some_terms, 0)
    outgoing = exact_dot(slot_block.astype(BF16), terms[...])
    for c in range(CAP):
        term_out[:, 0, pl.ds(c * patch_width, patch_width)] = outgoing[c * n_x : (c + 1) * n_x]
    sent_term = send_all(term_out, term_in, 2)
    sent_term.wait()
    returned = jnp.concatenate(
        [term_in[:, 0, pl.ds(c * patch_width, patch_width)] for c in range(CAP)], axis=0
    )

    asked_cols = jnp.concatenate(
        [asked, jnp.full((LANES - slots, LANES), -1.0, F32)], axis=0
    ).T[:rows, :slots]
    cell = row_iota((rows, slots)) * segs
    spread = jnp.concatenate(
        [
            jnp.where(asked_cols == (cell + (level * rows * segs + s)).astype(F32), 1.0, 0.0)
            for level in range(levels)
            for s in range(segs)
        ],
        axis=0,
    ).astype(BF16)
    forcing = exact_dot(spread, returned)
    for level in range(levels):
        for s in range(segs):
            start = (level * segs + s) * rows
            for v in range(VARS):
                plane = v * levels + level
                field_c[plane, s, own, :] = (
                    std[plane, s]
                    * forcing[start : start + rows, v * LANES : (v + 1) * LANES]
                )
    sent_x2 = send_x((field_c,), (x2_send, x2_recv))
    for side, t in ((0, 0), (1, segs - 1)):
        strip = jnp.zeros((rows, LANES), F32)
        for plane in range(planes):
            value = field_c[plane, t, own, :]
            shift = (plane * RIM + side * RIM) % LANES
            if shift:
                value = pltpu.roll(value, shift, 1)
            here = (strip_lane >= plane * RIM) & (strip_lane < (plane + 1) * RIM)
            strip = jnp.where(here, value, strip)
        strip_out2[side] = strip
    sent_y2 = send_y(strip_out2, strip_in2, (y2_send, y2_recv))
    for copy in sent_x2 + sent_y2:
        copy.wait()
    for plane in range(planes):
        field_c[plane, segs, ext, :] = unpack(strip_in2, plane)

    to_lanes(field_c, lane_a, range(planes))
    diffuse(lane_a, lane_b, lane_x, lane_y)
    from_lanes(lane_a, field_c, planes)

    stores = []
    for s in range(segs):
        for plane in range(planes):
            out_tile[plane, s] = sea[plane % levels, s, own, :] * field_c[plane, s, own, :]
        copy = pltpu.make_async_copy(
            out_tile.at[:, s, :, :],
            gradient.at[:, :, pl.ds(s * LANES, LANES)],
            load_sem.at[s],
        )
        copy.start()
        stores.append(copy)
    for copy in stores:
        copy.wait()


def finish(increment, control, departed, gradient, departures):
    gradient[...] = control[...] + increment[...]
    departures[...] = departed[...]


def body(
    n_x,
    n_y,
    control,
    background_std,
    kappa_x,
    kappa_y,
    sea_mask,
    obs_weights,
    obs_values,
    obs_rinv,
    obs_tile,
    obs_offset,
):
    planes, rows, cols = control.shape
    levels = kappa_x.shape[0]
    blocks, nobs, width = obs_weights.shape
    segs = cols // LANES
    height = rows + 4 * RIM
    inputs = planes + 2 * levels
    hbm = pl.BlockSpec(memory_space=pl.ANY)
    vmem = pl.BlockSpec(memory_space=pltpu.VMEM)
    dma = pltpu.SemaphoreType.DMA
    field = pltpu.VMEM((planes, segs + 1, height, LANES), F32)
    depth = height * planes * segs // LANES
    lanes = pltpu.VMEM((depth, height, LANES), F32)
    face = pltpu.VMEM((levels, segs + 1, height, LANES), F32)
    increment, departed = pl.pallas_call(
        functools.partial(kernel, n_x, n_y),
        out_shape=(
            jax.ShapeDtypeStruct(control.shape, F32),
            jax.ShapeDtypeStruct(obs_values.shape, F32),
        ),
        in_specs=[hbm] * 10,
        out_specs=(hbm, vmem),
        scratch_shapes=[
            pltpu.VMEM((inputs, segs, height, LANES), F32),
            pltpu.VMEM((levels, segs, height, LANES), jnp.int32),
            pltpu.VMEM((planes, segs, rows, LANES), F32),
            pltpu.VMEM((blocks, nobs, width), BF16),
            face,
            face,
            face,
            field,
            field,
            lanes,
            lanes,
            lanes,
            lanes,
            pltpu.VMEM((2, rows, LANES), F32),
            pltpu.VMEM((2, height, LANES), F32),
            pltpu.VMEM((2, rows, LANES), F32),
            pltpu.VMEM((2, height, LANES), F32),
            pltpu.VMEM((n_x, 1, CAP * LANES), F32),
            pltpu.VMEM((n_x, 1, CAP * LANES), F32),
            pltpu.VMEM((n_x, 1, CAP * width), F32),
            pltpu.VMEM((n_x, 1, CAP * width), F32),
            pltpu.VMEM((n_x, 1, CAP * width), F32),
            pltpu.VMEM((n_x, 1, CAP * width), F32),
            pltpu.VMEM((blocks, width), F32),
            pltpu.VMEM((planes, segs, rows, LANES), F32),
            pltpu.VMEM((blocks, nobs), F32),
            pltpu.VMEM((blocks, nobs), F32),
            pltpu.VMEM((1, blocks), jnp.int32),
            pltpu.VMEM((1, blocks), jnp.int32),
            dma((5 * segs + 5,)),
            dma((4,)),
            dma((4,)),
            dma((6,)),
            dma((6,)),
            dma((2,)),
            dma((2,)),
            dma((6,)),
            dma((6,)),
            dma((3,)),
            dma((3,)),
        ],
        compiler_params=pltpu.CompilerParams(
            collective_id=0, has_side_effects=True, vmem_limit_bytes=66_000_000
        ),
        name="variational_gradient",
    )(
        control,
        background_std,
        kappa_x,
        kappa_y,
        sea_mask,
        obs_weights,
        obs_values,
        obs_rinv,
        obs_tile.reshape(1, blocks),
        obs_offset.reshape(1, blocks),
    )
    slab = pl.BlockSpec((1, rows, cols), lambda plane: (plane, 0, 0))
    whole = pl.BlockSpec((blocks, nobs), lambda plane: (0, 0))
    return pl.pallas_call(
        finish,
        grid=(planes,),
        out_shape=(
            jax.ShapeDtypeStruct(control.shape, F32),
            jax.ShapeDtypeStruct(obs_values.shape, F32),
        ),
        in_specs=[slab, slab, whole],
        out_specs=(slab, whole),
        name="add_control",
    )(increment, control, departed)


def solution(mesh):
    grid = P(None, "gx", "gy")
    holder = ("gx", "gy")
    in_specs = (
        grid,
        grid,
        grid,
        grid,
        grid,
        P(holder, None, None),
        P(holder, None),
        P(holder, None),
        P(holder, None),
        P(holder),
    )
    return jax.shard_map(
        functools.partial(body, mesh.shape["gx"], mesh.shape["gy"]),
        mesh=mesh,
        in_specs=in_specs,
        out_specs=(grid, P(holder, None)),
        check_vma=False,
    )
```
